32 devices in a mesh: dp: 8 (over y, x, core), fsdp: 4 (over z).
Axes of the slice: x: 2, y: 2, z: 4, core: 2. Of those that a mesh axis runs over, the one named last changes fastest.
Arguments:
- glu_frames: bfloat16 [8192, 1536], P(('dp', 'fsdp')), may hold values from -6 to 6
- residual_frames: bfloat16 [8192, 1536], P(('dp', 'fsdp')), may hold values from -6 to 6
- send_rows: int32 [8, 4, 8, 32], P('dp', 'fsdp'), may hold values from 0 to 255, as said below
- recv_slot: int32 [8, 4, 128], P('dp', 'fsdp'), may hold values from 0 to 255, as said below
- segment_ids: int32 [8, 4, 128], P('dp', 'fsdp'), may hold values from 0 to 15, never falling along the last dimension, each value on 1 to 64 neighbouring positions
- code_targets: int32 [8, 512], P('dp'), may hold values from 0 to 8191
- conv_kernel: float32 [31, 1536], replicated, may hold values from -1 to 1
- norm_gain: float32 [1536], replicated, may hold values from 0.5 to 1.5
- point_weight: bfloat16 [1536, 1536], P('fsdp'), may hold values from -0.15625 to 0.15625
- code_head: bfloat16 [1536, 8192], P(None, 'fsdp')
Outputs:
- loss: float32 [], replicated
- grad_head: float32 [1536, 8192], P('dp', 'fsdp')
- grad_point: float32 [1536, 1536], P('fsdp', 'dp')
- grad_kernel: float32 [31, 1536], replicated
- grad_gain: float32 [1536], replicated
- grad_residual: bfloat16 [4096, 1536], P(('dp', 'fsdp'))
- grad_glu: bfloat16 [4096, 1536], P(('dp', 'fsdp'))
The draws below stay inside these ranges and needn't reach their ends.
Inputs may be any that keep to these rules, and one draw needn't show every extreme that they name: send_rows[i, f, o] lists 32 local slots of loading device (i, f) for owner (o, f). Each loading device fills whole buckets for between 2 and 8 owners, at most one bucket per owner, with distinct slots; its entries for other owners are never read. recv_slot[o, f, r] = i * 32 + c names position c of the bucket from loading device (i, f). Each owner reads 4 full buckets of 32 frames, from distinct loading devices, each whole and in order.
All inputs are finite; a program needn't handle non-finite values.
Results may differ from the reference program's by a relative error of at most 0.012.
The reference program's roundings to bfloat16 on the way (of `glu_owned`, `residual_owned`, `activation`, `residual_new` and `logit_grad`) count: a program that leaves them out, or rounds other values in their place, can miss the bound.
Values may be sent and summed in bfloat16 or wider, within the bound.
No kernel may reach another device: no remote copies, remote signals or barrier semaphores. Data moves between devices by JAX's collectives and lax.ppermute only.
A program may use at most 128 MiB of HBM per device.

```python
import math
import jax
import jax.numpy as jnp
import numpy as np
from jax import lax

D = 1536
CODES = 8192
K = 31
ROWS_DEV = 128
PIECES = 4
CAP = 32
LOAD_DEV = 256
TOTAL = 4096
N_DP = 8
N_FSDP = 4


def routing_tables(key):
    quarter = N_DP // 4
    counts = np.array([2 * PIECES] * quarter + [PIECES] * quarter + [PIECES // 2] * (N_DP - 2 * quarter))
    entries = PIECES * N_DP
    base_loader = np.repeat(np.arange(N_DP), counts)
    run_start = np.cumsum(counts) - counts
    piece_slot = np.arange(entries) - np.repeat(run_start, counts)
    piece_index = np.arange(entries) // N_DP
    owner_pos = np.arange(entries) % N_DP
    slot_total = LOAD_DEV // CAP

    def shuffle_slots(sub_key):
        return jax.random.permutation(sub_key, slot_total).astype(jnp.int32)

    def one_group(group_key):
        key_list = jax.random.split(group_key, 4)
        loader_perm = jax.random.permutation(key_list[0], N_DP).astype(jnp.int32)
        owner_perm = jax.random.permutation(key_list[1], N_DP).astype(jnp.int32)
        slot_perm = jax.vmap(shuffle_slots)(jax.random.split(key_list[2], N_DP))
        loaders = loader_perm[base_loader]
        owners = owner_perm[owner_pos]
        slot_ids = slot_perm[loaders, piece_slot]
        within = jnp.arange(CAP, dtype=jnp.int32)
        send_table = jax.random.randint(key_list[3], (N_DP, N_DP, CAP), 0, LOAD_DEV, dtype=jnp.int32)
        send_table = send_table.at[loaders, owners].set(slot_ids[:, None] * CAP + within[None, :])
        recv_table = jnp.zeros((N_DP, PIECES, CAP), jnp.int32).at[owners, piece_index].set(loaders[:, None] * CAP + within[None, :])
        return (send_table, recv_table.reshape(N_DP, ROWS_DEV))
    send_table, recv_table = jax.vmap(one_group)(jax.random.split(key, N_FSDP))
    return (jnp.transpose(send_table, (1, 0, 2, 3)), jnp.transpose(recv_table, (1, 0, 2)))


def draw_send_rows(key, part):
    return routing_tables(jax.random.fold_in(key, 11))[0]


def draw_recv_slot(key, part):
    return routing_tables(jax.random.fold_in(key, 11))[1]


def draw_code_head(key, part):
    key_list = jax.random.split(key, 2)
    base = jax.random.normal(key_list[0], (D, CODES), jnp.float32) * D ** (-0.5)
    col_scale = jnp.exp(jax.random.uniform(key_list[1], (1, CODES), jnp.float32, jnp.log(0.5), jnp.log(8.0)))
    return (base * col_scale).astype(jnp.bfloat16)


def with_ends(result, stream_key, smallest, high):
    place = [jax.random.randint(jax.random.fold_in(stream_key, axis), (), 0, length) for axis, length in enumerate(result.shape)]
    widest = result.shape.index(max(result.shape))
    beside = place[:widest] + [(place[widest] + 1) % result.shape[widest]] + place[widest + 1:]
    return result.at[tuple(place)].set(smallest).at[tuple(beside)].set(high)


def shard_levels(key, dims, shards, smallest, largest):
    loudness, own = 1.0, jax.random.fold_in(key, 6)
    for position, parts in shards:
        draws = jnp.exp(jax.random.uniform(jax.random.fold_in(own, position), (parts,), jnp.float32, smallest / len(shards), largest / len(shards)))
        loudness = loudness * jnp.repeat(draws, dims[position] // parts).reshape([-1 if axis == position else 1 for axis in range(len(dims))])
    return loudness


def profile(number_of, total, limit, skew):
    loads = [(1 << 20) // math.isqrt(standing ** skew) + 1 for standing in range(2, number_of + 1)]
    spare, holding = total - limit - (number_of - 1), [1] * (number_of - 1)
    while spare > 0:
        free = [i for i in range(number_of - 1) if holding[i] < limit]
        pool, remaining = sum([loads[i] for i in free]), spare
        for i in free:
            addition = min(limit - holding[i], max(1, remaining * loads[i] // pool), spare)
            holding[i] = holding[i] + addition
            spare = spare - addition
    return np.array([limit] + holding)


def uneven(own_key, count, total, reach, slope):
    if count == 2:
        one = jax.random.randint(own_key, (), max(1, total - reach), min(reach, total - 1) + 1)
        return jnp.stack([one, total - one])
    tallies = jnp.asarray(profile(count, total, reach, slope), jnp.int32)
    pairs = (count - 1) // 2
    donor, sink = tallies[1:1 + 2 * pairs:2], tallies[2:2 + 2 * pairs:2]
    room = jnp.minimum(donor - 1, reach - sink)
    moved = jax.random.randint(jax.random.fold_in(own_key, 1), (pairs,), 0, 1 << 20) % (room + 1)
    tallies = tallies.at[1:1 + 2 * pairs:2].set(donor - moved).at[2:2 + 2 * pairs:2].set(sink + moved)
    return tallies[jax.random.permutation(jax.random.fold_in(own_key, 2), count)]


def noise(rng, dims, spread, reach, shards=(), kind=jnp.bfloat16):
    loudness = shard_levels(rng, dims, shards, -0.22, 0.18) if shards else 1.0
    values = jax.random.normal(rng, dims, jnp.float32) * spread * loudness
    return jnp.minimum(jnp.maximum(values, -reach), reach).astype(kind)


def setup_inputs(seed: int = 0) -> dict:
    arg_keys = jax.random.split(jax.random.key(seed), 11)
    glu_frames = noise(arg_keys[0], (LOAD_DEV * N_DP * N_FSDP, D), 1.0, 6.0, ((0, 32),))
    residual_frames = noise(arg_keys[1], (LOAD_DEV * N_DP * N_FSDP, D), 1.0, 6.0, ((0, 32),))
    send_rows = draw_send_rows(jax.random.fold_in(arg_keys[10], 71), 0)
    recv_slot = draw_recv_slot(jax.random.fold_in(arg_keys[10], 71), 0)
    segment_ids = jax.vmap(lambda own: jnp.searchsorted(jnp.cumsum(uneven(own, ROWS_DEV // 8, ROWS_DEV, ROWS_DEV // 2, 0)), jnp.arange(ROWS_DEV), side="right"))(jax.random.split(arg_keys[4], N_DP * N_FSDP)).reshape((N_DP, N_FSDP, ROWS_DEV)).astype(jnp.int32)
    code_targets = with_ends(jax.random.randint(arg_keys[5], (N_DP, N_FSDP * ROWS_DEV), 0, CODES), jax.random.fold_in(arg_keys[5], 1), 0, CODES - 1).astype(jnp.int32)
    conv_kernel = noise(arg_keys[6], (K, D), K ** -0.5, 1.0, (), jnp.float32)
    norm_gain = jnp.clip(1.0 + 0.1 * jax.random.normal(arg_keys[7], (D,), jnp.float32), 0.5, 1.5)
    point_weight = noise(arg_keys[8], (D, D), D ** -0.5, 0.15625, ((0, 4),))
    code_head = draw_code_head(jax.random.fold_in(arg_keys[10], 71), 0)
    return dict(glu_frames=glu_frames, residual_frames=residual_frames, send_rows=send_rows, recv_slot=recv_slot, segment_ids=segment_ids, code_targets=code_targets, conv_kernel=conv_kernel, norm_gain=norm_gain, point_weight=point_weight, code_head=code_head)


def route_rows(frames, send_rows, recv_slot):
    loader = frames.reshape(N_DP, N_FSDP, LOAD_DEV, D)
    source = recv_slot // CAP
    within = recv_slot % CAP
    group_idx = jnp.arange(N_FSDP, dtype=jnp.int32)[None, :, None]
    owner_idx = jnp.arange(N_DP, dtype=jnp.int32)[:, None, None]
    picked = send_rows[source, group_idx, owner_idx, within]
    return loader[source, group_idx, picked].reshape(TOTAL, D)

def reference(glu_frames, residual_frames, send_rows, recv_slot, segment_ids, code_targets, conv_kernel, norm_gain, point_weight, code_head):
    half_taps = K // 2
    blocks = N_DP * N_FSDP
    glu_owned = route_rows(glu_frames, send_rows, recv_slot)
    residual_owned = route_rows(residual_frames, send_rows, recv_slot)
    segments = segment_ids.reshape(blocks, ROWS_DEV)
    seg_pad = jnp.pad(segments, ((0, 0), (half_taps, half_taps)), constant_values=-1)
    glu_pad = jnp.pad(glu_owned.astype(jnp.float32).reshape(blocks, ROWS_DEV, D), ((0, 0), (half_taps, half_taps), (0, 0)))
    conv_out = jnp.zeros((blocks, ROWS_DEV, D), jnp.float32)
    for offset in range(K):
        same_seg = (seg_pad[:, offset:offset + ROWS_DEV] == segments)[:, :, None]
        conv_out = conv_out + conv_kernel[offset] * jnp.where(same_seg, glu_pad[:, offset:offset + ROWS_DEV], 0.0)
    conv_out = conv_out.reshape(TOTAL, D)
    centred = conv_out - lax.optimization_barrier(jnp.mean(conv_out, axis=1, keepdims=True))
    inv_std = lax.rsqrt(lax.optimization_barrier(jnp.mean(centred * centred, axis=1, keepdims=True)) + 1e-05)
    standard = centred * inv_std
    normed = standard * norm_gain
    gate_sig = jax.nn.sigmoid(normed)
    activation = (normed * gate_sig).astype(jnp.bfloat16)
    branch = jnp.dot(activation, point_weight, preferred_element_type=jnp.float32)
    residual_new = (residual_owned.astype(jnp.float32) + branch).astype(jnp.bfloat16)
    block_rows = N_FSDP * ROWS_DEV

    def head_block(state_in, inputs):
        head_grad, loss_sum = state_in
        rows_in, targets = inputs
        logits = jnp.dot(rows_in, code_head, preferred_element_type=jnp.float32)
        row_top = lax.optimization_barrier(jnp.max(logits, axis=1))
        log_norm = row_top + jnp.log(lax.optimization_barrier(jnp.sum(jnp.exp(logits - row_top[:, None]), axis=1)))
        target_hits = targets[:, None] == jnp.arange(CODES, dtype=jnp.int32)[None, :]
        row_pick = lax.optimization_barrier(jnp.sum(jnp.where(target_hits, logits, 0.0), axis=1))
        loss_sum = loss_sum + jnp.sum(log_norm - row_pick)
        logit_grad = (jnp.exp(logits - log_norm[:, None]) - target_hits.astype(jnp.float32)).astype(jnp.bfloat16)
        head_grad = head_grad + jnp.dot(rows_in.T, logit_grad, preferred_element_type=jnp.float32)
        frame_grad = jnp.dot(logit_grad, code_head.T, preferred_element_type=jnp.float32).astype(jnp.bfloat16)
        return ((head_grad, loss_sum), frame_grad)
    start_state = (jnp.zeros((D, CODES), jnp.float32), jnp.zeros((), jnp.float32))
    (grad_head, loss_sum), grad_residual = lax.scan(head_block, start_state, (residual_new.reshape(-1, block_rows, D), code_targets.reshape(-1, block_rows)))
    grad_residual = grad_residual.reshape(TOTAL, D)
    grad_point = jnp.dot(activation.T, grad_residual, preferred_element_type=jnp.float32)
    act_grad = jnp.dot(grad_residual, point_weight.T, preferred_element_type=jnp.float32)
    normed_grad = act_grad * gate_sig * (1.0 + normed * (1.0 - gate_sig))
    grad_gain = lax.optimization_barrier(jnp.sum(normed_grad * standard, axis=0))
    scaled = normed_grad * norm_gain
    conv_grad = inv_std * (scaled - lax.optimization_barrier(jnp.mean(scaled, axis=1, keepdims=True)) - standard * lax.optimization_barrier(jnp.mean(scaled * standard, axis=1, keepdims=True)))
    conv_grad = conv_grad.reshape(blocks, ROWS_DEV, D)
    kernel_rows = []
    for offset in range(K):
        same_seg = (seg_pad[:, offset:offset + ROWS_DEV] == segments)[:, :, None]
        kernel_rows.append(lax.optimization_barrier(jnp.sum(conv_grad * jnp.where(same_seg, glu_pad[:, offset:offset + ROWS_DEV], 0.0), axis=(0, 1))))
    grad_kernel = jnp.stack(kernel_rows)
    grad_pad = jnp.pad(conv_grad, ((0, 0), (half_taps, half_taps), (0, 0)))
    glu_grad = jnp.zeros((blocks, ROWS_DEV, D), jnp.float32)
    for offset in range(K):
        begin_row = 2 * half_taps - offset
        same_seg = (seg_pad[:, begin_row:begin_row + ROWS_DEV] == segments)[:, :, None]
        glu_grad = glu_grad + conv_kernel[offset] * jnp.where(same_seg, grad_pad[:, begin_row:begin_row + ROWS_DEV], 0.0)
    grad_glu = glu_grad.reshape(TOTAL, D).astype(jnp.bfloat16)
    return (loss_sum / TOTAL, grad_head, grad_point, grad_kernel, grad_gain, grad_residual, grad_glu)
```

```python
import jax
import jax.numpy as jnp
from jax import lax
from jax.sharding import PartitionSpec as P

F32 = jnp.float32
BF16 = jnp.bfloat16


def flip_dp(value, mask):
    count = lax.axis_size("dp")
    return lax.ppermute(value, "dp", [(i, i ^ mask) for i in range(count)])


def flip_fsdp(value, mask):
    count = lax.axis_size("fsdp")
    return lax.ppermute(value, "fsdp", [(i, i ^ mask) for i in range(count)])


def shift_fsdp(value, step):
    count = lax.axis_size("fsdp")
    return lax.ppermute(value, "fsdp", [(i, (i + step) % count) for i in range(count)])


def pick(array, index, axis=0):
    return lax.dynamic_index_in_dim(array, index, axis, keepdims=False)


def ordered(bit, own, other, axis):
    return jnp.where(
        bit == 0, jnp.stack([own, other], axis), jnp.stack([other, own], axis)
    )


def tree_sum(values):
    while len(values) > 1:
        values = [values[i] + values[i + 1] for i in range(0, len(values), 2)]
    return values[0]


def gather_point(point_weight, d, f):
    count = lax.axis_size("fsdp")
    rows, width = point_weight.shape
    core, bit1, bit2 = d & 1, (d >> 1) & 1, (d >> 2) & 1
    parts = point_weight.reshape(2, 2, 2, rows // 8, width)
    piece1 = pick(pick(parts[0], bit1), core)
    piece2 = pick(pick(parts[1], bit2), core)
    piece = jnp.stack([piece1, piece2])
    got = jnp.stack([shift_fsdp(piece, step) for step in range(1, count)])
    first, second = got[:, 0], got[:, 1]
    half1 = ordered(bit1, first, flip_dp(first, 2), 1)
    half2 = ordered(bit2, second, flip_dp(second, 4), 1)
    mine = jnp.stack([half1, half2], 1)
    whole = ordered(core, mine, flip_dp(mine, 1), 3).reshape(count - 1, rows, width)
    panel = jnp.zeros((count, rows, width), point_weight.dtype)
    panel = lax.dynamic_update_index_in_dim(panel, point_weight, f, 0)
    for step in range(1, count):
        panel = lax.dynamic_update_index_in_dim(panel, whole[step - 1], (f - step) % count, 0)
    return panel.reshape(count * rows, width)


def gather_rows(own, f):
    count = lax.axis_size("fsdp")
    if count != 4:
        return [(0, own)] + [(count - step, shift_fsdp(own, step)) for step in range(1, count)]
    before = shift_fsdp(own, 1)
    after = shift_fsdp(own, -1)
    source = jnp.where(f == 2, before, jnp.where(f == 1, after, own))
    across = lax.ppermute(source, "fsdp", [(0, 2), (3, 1), (2, 3), (1, 0)])
    return [(0, own), (3, before), (1, after), (2, across)]


def scatter_rows(blocks, f):
    count = lax.axis_size("fsdp")
    if count != 4:
        total = blocks[0]()
        for step in range(1, count):
            total = total + shift_fsdp(blocks[step]().astype(BF16), step).astype(F32)
        return total
    across = lax.ppermute(
        blocks[2]().astype(BF16), "fsdp", [(2, 0), (1, 3), (3, 2), (0, 1)]
    ).astype(F32)
    ahead, behind = blocks[1](), blocks[3]()
    ahead = ahead + jnp.where(f == 1, across, 0.0)
    behind = behind + jnp.where(f == 2, across, 0.0)
    got1 = shift_fsdp(ahead.astype(BF16), 1).astype(F32)
    got2 = shift_fsdp(behind.astype(BF16), -1).astype(F32)
    direct = jnp.where((f == 0) | (f == 3), across, 0.0)
    return blocks[0]() + direct + got1 + got2


def reduce_head(head, d):
    count = lax.axis_size("dp")
    bits = count.bit_length() - 1
    rows, width = head.shape
    cut = head.reshape(*([2] * bits), rows // count, width)

    def halve(value, left, bit):
        axis = left.index(bit)
        mine = (d >> bit) & 1
        sent = flip_dp(pick(value, 1 - mine, axis), 1 << bit)
        total = pick(value, mine, axis).astype(F32) + sent.astype(F32)
        return total, [b for b in left if b != bit]

    left = list(range(bits - 1, -1, -1))
    total, left = halve(cut, left, 0)
    total = total.astype(BF16)
    half = width // 2
    sides = [(total[..., :half], left), (total[..., half:], left)]
    orders = [list(range(1, bits)), list(range(bits - 1, 0, -1))]
    for step in range(bits - 1):
        sides = [halve(v.astype(BF16), l, o[step]) for (v, l), o in zip(sides, orders)]
    return jnp.concatenate([v for v, _ in sides], axis=-1)


def local(
    glu_frames,
    residual_frames,
    send_rows,
    recv_slot,
    segment_ids,
    code_targets,
    conv_kernel,
    norm_gain,
    point_weight,
    code_head,
):
    n_dp, n_fsdp = lax.axis_size("dp"), lax.axis_size("fsdp")
    d, f = lax.axis_index("dp"), lax.axis_index("fsdp")
    feature_width = glu_frames.shape[1]
    tap_count = conv_kernel.shape[0]
    half_taps = tap_count // 2
    slot_list = recv_slot[0, 0]
    row_count = slot_list.shape[0]
    picked_rows = send_rows[0, 0]

    glu_sent = glu_frames[picked_rows]
    glu_recv = lax.all_to_all(glu_sent, "dp", split_axis=0, concat_axis=0, tiled=True)
    full_panel = gather_point(point_weight, d, f)
    residual_sent = residual_frames[picked_rows]
    residual_recv = lax.all_to_all(residual_sent, "dp", split_axis=0, concat_axis=0, tiled=True)

    glu_owned = glu_recv.reshape(-1, feature_width)[slot_list]
    residual_owned = residual_recv.reshape(-1, feature_width)[slot_list]
    segments = segment_ids[0, 0]
    seg_pad = jnp.pad(segments, (half_taps, half_taps), constant_values=-1)
    glu_pad = jnp.pad(glu_owned.astype(F32), ((half_taps, half_taps), (0, 0)))
    conv_out = jnp.zeros((row_count, feature_width), F32)
    kept_list = []
    for offset in range(tap_count):
        same_seg = (seg_pad[offset : offset + row_count] == segments)[:, None]
        kept = jnp.where(same_seg, glu_pad[offset : offset + row_count], 0.0)
        kept_list.append(kept)
        conv_out = conv_out + conv_kernel[offset] * kept
    centred = conv_out - jnp.mean(conv_out, axis=1, keepdims=True)
    inv_std = lax.rsqrt(jnp.mean(centred * centred, axis=1, keepdims=True) + 1e-05)
    standard = centred * inv_std
    normed = standard * norm_gain
    gate_sig = jax.nn.sigmoid(normed)
    activation = (normed * gate_sig).astype(BF16)

    branch_out = jnp.dot(activation, full_panel, preferred_element_type=F32)
    residual_new = (residual_owned.astype(F32) + branch_out).astype(BF16)

    code_local = code_head.shape[1]
    targets = code_targets[0].reshape(n_fsdp, row_count) - f * code_local
    columns = lax.broadcasted_iota(jnp.int32, (1, code_local), 1)
    gathered = gather_rows(residual_new, f)
    logits, hits, stats = {}, {}, {}
    for distance, block in gathered:
        logits[distance] = jnp.dot(block, code_head, preferred_element_type=F32)
        hits[distance] = pick(targets, (f + distance) % n_fsdp)[:, None] == columns
        top = jnp.max(logits[distance], axis=1)
        total = jnp.sum(jnp.exp(logits[distance] - top[:, None]), axis=1)
        chosen = jnp.sum(jnp.where(hits[distance], logits[distance], 0.0), axis=1)
        stats[distance] = jnp.stack([top, total, chosen])
    act_even = [activation] + [flip_dp(activation, mask) for mask in range(2, n_dp, 2)]
    act_even = jnp.concatenate(act_even)
    act_odd = flip_dp(act_even, 1)
    table = jnp.zeros((n_fsdp, 3, row_count), F32)
    for distance, _ in gathered:
        table = lax.dynamic_update_index_in_dim(
            table, stats[distance], (f + distance) % n_fsdp, 0
        )
    tables = [table] + [flip_fsdp(table, mask) for mask in range(1, n_fsdp)]
    tops = tables[0][:, 0]
    for other in tables[1:]:
        tops = jnp.maximum(tops, other[:, 0])
    sums = tree_sum([t[:, 1] * jnp.exp(t[:, 0] - tops) for t in tables])
    log_norm = tops + jnp.log(sums)
    loss_part = jnp.sum(log_norm - tree_sum([t[:, 2] for t in tables]))

    def logit_grad(distance):
        norm = pick(log_norm, (f + distance) % n_fsdp)[:, None]
        return (jnp.exp(logits[distance] - norm) - hits[distance].astype(F32)).astype(BF16)

    grads = {distance: logit_grad(distance) for distance, _ in gathered}

    def row_grad(distance):
        return lambda: lax.dot_general(
            grads[distance], code_head, (((1,), (1,)), ((), ())), preferred_element_type=F32
        )

    grad_residual = scatter_rows(
        {distance: row_grad(distance) for distance, _ in gathered}, f
    ).astype(BF16)

    all_rows = jnp.concatenate([block for _, block in gathered])
    all_grads = jnp.concatenate([grads[distance] for distance, _ in gathered])
    head_local = lax.dot_general(
        all_rows, all_grads, (((0,), (0,)), ((), ())), preferred_element_type=F32
    ).astype(BF16)
    grad_head = reduce_head(head_local, d)

    part_width = feature_width // n_dp
    cols = lax.all_to_all(
        grad_residual.reshape(row_count, n_dp, part_width).transpose(1, 0, 2),
        "dp",
        split_axis=0,
        concat_axis=0,
        tiled=True,
    )
    bits = n_dp.bit_length() - 1
    cols = cols.reshape(*([2] * bits), row_count, part_width)
    for bit in range(bits):
        axis = bits - 1 - bit
        cols = jnp.where((d >> bit) & 1 == 1, jnp.flip(cols, axis), cols)
    cols = jnp.moveaxis(cols, bits - 1, 0)
    act_all = jnp.concatenate([act_even, act_odd])
    point_part = lax.dot_general(
        act_all,
        cols.reshape(n_dp * row_count, part_width),
        (((0,), (0,)), ((), ())),
        preferred_element_type=F32,
    ).reshape(n_fsdp, feature_width // n_fsdp, part_width)
    point_sent = point_part.astype(BF16)
    grad_point = tree_sum(
        [pick(point_part, f)]
        + [
            flip_fsdp(pick(point_sent, f ^ mask), mask).astype(F32)
            for mask in range(1, n_fsdp)
        ]
    )

    act_grad = lax.dot_general(
        grad_residual, full_panel, (((1,), (1,)), ((), ())), preferred_element_type=F32
    )
    normed_grad = act_grad * gate_sig * (1.0 + normed * (1.0 - gate_sig))
    gain_grad = jnp.sum(normed_grad * standard, axis=0)
    scaled = normed_grad * norm_gain
    conv_grad = inv_std * (
        scaled
        - jnp.mean(scaled, axis=1, keepdims=True)
        - standard * jnp.mean(scaled * standard, axis=1, keepdims=True)
    )
    kernel_grad = [jnp.sum(conv_grad * kept, axis=0) for kept in kept_list]
    grad_pad = jnp.pad(conv_grad, ((half_taps, half_taps), (0, 0)))
    glu_grad = jnp.zeros((row_count, feature_width), F32)
    for offset in range(tap_count):
        begin_row = 2 * half_taps - offset
        same_seg = (seg_pad[begin_row : begin_row + row_count] == segments)[:, None]
        glu_grad = glu_grad + conv_kernel[offset] * jnp.where(
            same_seg, grad_pad[begin_row : begin_row + row_count], 0.0
        )

    core = d & 1
    packet = jnp.stack(kernel_grad + [gain_grad]).reshape(2, -1, feature_width)
    packet = pick(packet, core) + flip_dp(pick(packet, 1 - core).astype(BF16), 1).astype(F32)
    packet = packet.astype(BF16)
    packet = tree_sum(
        [packet.astype(F32)]
        + [flip_dp(packet, mask).astype(F32) for mask in range(2, n_dp, 2)]
    )
    packet = packet.astype(BF16)
    packet = tree_sum(
        [packet.astype(F32)]
        + [flip_fsdp(packet, mask).astype(F32) for mask in range(1, n_fsdp)]
    )
    packet = ordered(core, packet, flip_dp(packet, 1), 0).reshape(-1, feature_width)

    loss_sum = loss_part.reshape(1, 1)
    for bit in range(n_dp.bit_length() - 1):
        loss_sum = loss_sum + flip_dp(loss_sum, 1 << bit)
    loss = loss_sum[0, 0] / (row_count * n_dp * n_fsdp)
    return (
        loss,
        grad_head,
        grad_point,
        packet[:tap_count],
        packet[tap_count],
        grad_residual,
        glu_grad.astype(BF16),
    )


def solution(mesh):
    placed = (
        P(("dp", "fsdp"), None),
        P(("dp", "fsdp"), None),
        P("dp", "fsdp", None, None),
        P("dp", "fsdp", None),
        P("dp", "fsdp", None),
        P("dp", None),
        P(),
        P(),
        P("fsdp", None),
        P(None, "fsdp"),
    )
    return jax.shard_map(
        local,
        mesh=mesh,
        in_specs=placed,
        out_specs=(
            P(),
            P("dp", "fsdp"),
            P("fsdp", "dp"),
            P(),
            P(),
            P(("dp", "fsdp"), None),
            P(("dp", "fsdp"), None),
        ),
        check_vma=False,
    )
```

```python
import functools

import jax
import jax.numpy as jnp
from jax import lax
from jax.experimental import pallas as pl
from jax.experimental.pallas import tpu as pltpu
from jax.sharding import PartitionSpec as P

F32 = jnp.float32
BF16 = jnp.bfloat16


def flip_dp(value, mask):
    count = lax.axis_size("dp")
    return lax.ppermute(value, "dp", [(i, i ^ mask) for i in range(count)])


def flip_fsdp(value, mask):
    count = lax.axis_size("fsdp")
    return lax.ppermute(value, "fsdp", [(i, i ^ mask) for i in range(count)])


def shift_fsdp(value, step):
    count = lax.axis_size("fsdp")
    return lax.ppermute(value, "fsdp", [(i, (i + step) % count) for i in range(count)])


def pick(array, index, axis=0):
    return lax.dynamic_index_in_dim(array, index, axis, keepdims=False)


def ordered(bit, own, other, axis):
    return jnp.where(
        bit == 0, jnp.stack([own, other], axis), jnp.stack([other, own], axis)
    )


def tree_sum(values):
    while len(values) > 1:
        values = [values[i] + values[i + 1] for i in range(0, len(values), 2)]
    return values[0]


def after(value, *others):
    return lax.optimization_barrier((value, *others))[0]


def gather_point(point_weight, d):
    count = lax.axis_size("fsdp")
    rows, width = point_weight.shape
    core, bit1, bit2 = d & 1, (d >> 1) & 1, (d >> 2) & 1
    parts = point_weight.reshape(2, 2, 2, rows // 8, width)
    piece1 = pick(pick(parts[0], bit1), core)
    piece2 = pick(pick(parts[1], bit2), core)
    piece = jnp.stack([piece1, piece2])
    got = jnp.stack([shift_fsdp(piece, step) for step in range(1, count)], 1)
    across = [flip_dp(got[0], 2), flip_dp(got[1], 4)]
    near = [got] + across
    return near + [flip_dp(piece, 1) for piece in near]


def branch_kernel(
    place, weight, act, residual, got, got1, got2, far, far1, far2, panel, out, sems
):
    count = panel.shape[0]
    d, f = place[0], place[1]
    core, bits = d & 1, ((d >> 1) & 1, (d >> 2) & 1)
    copies = [(weight, panel.at[f])]
    for step in range(1, count):
        shard = panel.at[lax.rem(f + count - step, count)]
        for mine, others, side in (
            (got, (got1, got2), core),
            (far, (far1, far2), 1 - core),
        ):
            for half in range(2):
                copies.append((mine.at[half, step - 1], shard.at[half, bits[half], side]))
                copies.append((others[half].at[step - 1], shard.at[half, 1 - bits[half], side]))
    copies = [
        pltpu.make_async_copy(source, target, sems.at[i])
        for i, (source, target) in enumerate(copies)
    ]
    for copy in copies:
        copy.start()
    for copy in copies:
        copy.wait()
    rows, width = act.shape
    tile = 512
    whole = panel.reshape(act.shape[1], width)

    @pl.loop(0, width // tile)
    def _(step):
        lanes = pl.ds(pl.multiple_of(step * tile, tile), tile)
        total = jnp.dot(act[...], whole[:, lanes], preferred_element_type=F32)
        out[:, lanes] = (residual[:, lanes].astype(F32) + total).astype(BF16)


def branch(point_weight, activation, residual_owned, pieces, d, f):
    count = lax.axis_size("fsdp")
    rows, width = point_weight.shape
    vmem = pl.BlockSpec(memory_space=pltpu.VMEM)
    panel, out = pl.pallas_call(
        branch_kernel,
        out_shape=(
            jax.ShapeDtypeStruct((count, 2, 2, 2, rows // 8, width), BF16),
            jax.ShapeDtypeStruct(activation.shape, BF16),
        ),
        in_specs=[pl.BlockSpec(memory_space=pltpu.SMEM), pl.BlockSpec(memory_space=pl.ANY)]
        + [vmem] * 2
        + [pl.BlockSpec(memory_space=pl.ANY)] * 6,
        out_specs=(vmem, vmem),
        scratch_shapes=[pltpu.SemaphoreType.DMA((1 + 8 * (count - 1),))],
        compiler_params=pltpu.CompilerParams(vmem_limit_bytes=40 << 20),
        name="branch",
    )(
        jnp.stack([d, f]),
        point_weight.reshape(2, 2, 2, rows // 8, width),
        activation,
        residual_owned,
        *pieces,
    )
    return panel.reshape(count * rows, width), out


def point_kernel(count, place, cols, *refs):
    acts, out = refs[:count], refs[count]
    d, f = place[0], place[1]
    blocks, _, width = out.shape
    for block in range(blocks):
        lanes = slice(block * width, (block + 1) * width)
        total = jnp.zeros(out.shape[1:], F32)
        for mask in range(count):
            total = total + jnp.dot(
                cols[d ^ mask], acts[mask][:, lanes], preferred_element_type=F32
            )
        out[f ^ block] = total


def point_part(cols, acts, d, f):
    n_fsdp = lax.axis_size("fsdp")
    width = acts[0].shape[1] // n_fsdp
    vmem = pl.BlockSpec(memory_space=pltpu.VMEM)
    return pl.pallas_call(
        functools.partial(point_kernel, len(acts)),
        out_shape=jax.ShapeDtypeStruct((n_fsdp, cols.shape[1], width), F32),
        in_specs=[pl.BlockSpec(memory_space=pltpu.SMEM)] + [vmem] * (1 + len(acts)),
        out_specs=vmem,
        compiler_params=pltpu.CompilerParams(vmem_limit_bytes=40 << 20),
        name="point",
    )(jnp.stack([d, f]), cols, *acts)


def gather_rows(own, f):
    count = lax.axis_size("fsdp")
    if count != 4:
        return [(0, own)] + [(count - step, shift_fsdp(own, step)) for step in range(1, count)]
    before = shift_fsdp(own, 1)
    after = shift_fsdp(own, -1)
    source = jnp.where(f == 2, before, jnp.where(f == 1, after, own))
    across = lax.ppermute(source, "fsdp", [(0, 2), (3, 1), (2, 3), (1, 0)])
    return [(0, own), (3, before), (1, after), (2, across)]


def scatter_rows(blocks, f):
    count = lax.axis_size("fsdp")
    if count != 4:
        sent = [blocks[step]().astype(BF16) for step in range(1, count)]
        got = [shift_fsdp(value, step + 1).astype(F32) for step, value in enumerate(sent)]
        return sum(got, blocks[0]()), sent
    across = lax.ppermute(
        blocks[2]().astype(BF16), "fsdp", [(2, 0), (1, 3), (3, 2), (0, 1)]
    ).astype(F32)
    ahead, behind = blocks[1](), blocks[3]()
    ahead = ahead + jnp.where(f == 1, across, 0.0)
    behind = behind + jnp.where(f == 2, across, 0.0)
    ahead, behind = ahead.astype(BF16), behind.astype(BF16)
    got1 = shift_fsdp(ahead, 1).astype(F32)
    got2 = shift_fsdp(behind, -1).astype(F32)
    direct = jnp.where((f == 0) | (f == 3), across, 0.0)
    return blocks[0]() + direct + got1 + got2, [ahead, behind]


def halve(value, left, bit, d):
    axis = left.index(bit)
    mine = (d >> bit) & 1
    sent = flip_dp(pick(value, 1 - mine, axis), 1 << bit)
    total = pick(value, mine, axis).astype(F32) + sent.astype(F32)
    return total, [b for b in left if b != bit]


def halve_cores(head, d):
    count = lax.axis_size("dp")
    bits = count.bit_length() - 1
    rows, width = head.shape
    cut = head.reshape(*([2] * bits), rows // count, width)
    total, left = halve(cut, list(range(bits - 1, -1, -1)), 0, d)
    total = total.astype(BF16)
    return [(total[..., : width // 2], left), (total[..., width // 2 :], left)]


def halve_step(sides, d, step):
    bits = lax.axis_size("dp").bit_length() - 1
    orders = [list(range(1, bits)), list(range(bits - 1, 0, -1))]
    return [halve(v.astype(BF16), l, o[step], d) for (v, l), o in zip(sides, orders)]


def local(
    glu_frames,
    residual_frames,
    send_rows,
    recv_slot,
    segment_ids,
    code_targets,
    conv_kernel,
    norm_gain,
    point_weight,
    code_head,
):
    n_dp, n_fsdp = lax.axis_size("dp"), lax.axis_size("fsdp")
    d, f = lax.axis_index("dp"), lax.axis_index("fsdp")
    feature_width = glu_frames.shape[1]
    tap_count = conv_kernel.shape[0]
    half_taps = tap_count // 2
    slot_list = recv_slot[0, 0]
    row_count = slot_list.shape[0]
    picked_rows = send_rows[0, 0]

    glu_sent = glu_frames[picked_rows]
    glu_recv = lax.all_to_all(glu_sent, "dp", split_axis=0, concat_axis=0, tiled=True)
    pieces = gather_point(point_weight, d)
    residual_sent = after(residual_frames[picked_rows], glu_recv)
    residual_recv = lax.all_to_all(residual_sent, "dp", split_axis=0, concat_axis=0, tiled=True)

    glu_owned = glu_recv.reshape(-1, feature_width)[slot_list]
    residual_owned = residual_recv.reshape(-1, feature_width)[slot_list]
    segments = segment_ids[0, 0]
    seg_pad = jnp.pad(segments, (half_taps, half_taps), constant_values=-1)
    glu_pad = jnp.pad(glu_owned.astype(F32), ((half_taps, half_taps), (0, 0)))
    conv_out = jnp.zeros((row_count, feature_width), F32)
    kept_list = []
    for offset in range(tap_count):
        same_seg = (seg_pad[offset : offset + row_count] == segments)[:, None]
        kept = jnp.where(same_seg, glu_pad[offset : offset + row_count], 0.0)
        kept_list.append(kept)
        conv_out = conv_out + conv_kernel[offset] * kept
    centred = conv_out - jnp.mean(conv_out, axis=1, keepdims=True)
    inv_std = lax.rsqrt(jnp.mean(centred * centred, axis=1, keepdims=True) + 1e-05)
    standard = centred * inv_std
    normed = standard * norm_gain
    gate_sig = jax.nn.sigmoid(normed)
    activation = (normed * gate_sig).astype(BF16)

    full_panel, residual_new = branch(
        point_weight, activation, residual_owned, pieces, d, f
    )

    code_local = code_head.shape[1]
    targets = code_targets[0].reshape(n_fsdp, row_count) - f * code_local
    columns = lax.broadcasted_iota(jnp.int32, (1, code_local), 1)
    gathered = gather_rows(residual_new, f)
    logits, hits, stats = {}, {}, {}
    for distance, block in gathered:
        logits[distance] = jnp.dot(block, code_head, preferred_element_type=F32)
        hits[distance] = pick(targets, (f + distance) % n_fsdp)[:, None] == columns
        top = jnp.max(logits[distance], axis=1)
        total = jnp.sum(jnp.exp(logits[distance] - top[:, None]), axis=1)
        chosen = jnp.sum(jnp.where(hits[distance], logits[distance], 0.0), axis=1)
        stats[distance] = jnp.stack([top, total, chosen])
    act_own = after(activation, residual_new)
    acts = {mask: flip_dp(act_own, mask) if mask else act_own for mask in range(0, n_dp, 2)}
    acts.update({mask + 1: flip_dp(act, 1) for mask, act in list(acts.items())})
    places = jnp.arange(n_fsdp)[:, None, None]
    table = tree_sum(
        [
            jnp.where(places == (f + distance) % n_fsdp, stats[distance], 0.0)
            for distance, _ in gathered
        ]
    )
    tables = [table] + [flip_fsdp(table, mask) for mask in range(1, n_fsdp)]
    tops = tables[0][:, 0]
    for other in tables[1:]:
        tops = jnp.maximum(tops, other[:, 0])
    sums = tree_sum([t[:, 1] * jnp.exp(t[:, 0] - tops) for t in tables])
    log_norm = tops + jnp.log(sums)
    loss_part = jnp.sum(log_norm - tree_sum([t[:, 2] for t in tables]))

    def logit_grad(distance):
        norm = pick(log_norm, (f + distance) % n_fsdp)[:, None]
        return (jnp.exp(logits[distance] - norm) - hits[distance].astype(F32)).astype(BF16)

    loss_sum = loss_part.reshape(1, 1)
    for bit in range(n_dp.bit_length() - 1):
        loss_sum = loss_sum + flip_dp(loss_sum, 1 << bit)
    loss = loss_sum[0, 0] / (row_count * n_dp * n_fsdp)

    grads = {distance: logit_grad(distance) for distance, _ in gathered}

    def row_grad(distance, *others):
        return lambda: lax.dot_general(
            after(grads[distance], *others) if others else grads[distance],
            code_head,
            (((1,), (1,)), ((), ())),
            preferred_element_type=F32,
        )

    def all_parts(values):
        return jnp.concatenate([values[distance] for distance, _ in gathered])

    grad_residual, early = scatter_rows(
        {distance: row_grad(distance) for distance, _ in gathered}, f
    )
    grad_residual = grad_residual.astype(BF16)

    head_local = lax.dot_general(
        all_parts(dict(gathered)),
        after(all_parts(grads), *early),
        (((0,), (0,)), ((), ())),
        preferred_element_type=F32,
    ).astype(BF16)
    sides = halve_cores(head_local, d)

    part_width = feature_width // n_dp
    cols = lax.all_to_all(
        grad_residual.T.reshape(n_dp, part_width, row_count),
        "dp",
        split_axis=0,
        concat_axis=0,
        tiled=True,
    )
    sides = halve_step(sides, d, 0)
    cols = after(cols, *[v for v, _ in sides])
    point_sent = point_part(cols, [acts[mask] for mask in range(n_dp)], d, f)
    grad_point = tree_sum(
        [point_sent[0]]
        + [
            flip_fsdp(point_sent[mask].astype(BF16), mask).astype(F32)
            for mask in range(1, n_fsdp)
        ]
    ).T
    for step in range(1, n_dp.bit_length() - 2):
        sides = halve_step(sides, d, step)
    grad_head = jnp.concatenate([v for v, _ in sides], axis=-1)

    act_grad = lax.dot_general(
        grad_residual, full_panel, (((1,), (1,)), ((), ())), preferred_element_type=F32
    )
    normed_grad = act_grad * gate_sig * (1.0 + normed * (1.0 - gate_sig))
    gain_grad = jnp.sum(normed_grad * standard, axis=0)
    scaled = normed_grad * norm_gain
    conv_grad = inv_std * (
        scaled
        - jnp.mean(scaled, axis=1, keepdims=True)
        - standard * jnp.mean(scaled * standard, axis=1, keepdims=True)
    )
    kernel_grad = [jnp.sum(conv_grad * kept, axis=0) for kept in kept_list]
    grad_pad = jnp.pad(conv_grad, ((half_taps, half_taps), (0, 0)))
    glu_grad = jnp.zeros((row_count, feature_width), F32)
    for offset in range(tap_count):
        begin_row = 2 * half_taps - offset
        same_seg = (seg_pad[begin_row : begin_row + row_count] == segments)[:, None]
        glu_grad = glu_grad + conv_kernel[offset] * jnp.where(
            same_seg, grad_pad[begin_row : begin_row + row_count], 0.0
        )

    core = d & 1
    packet = jnp.stack(kernel_grad + [gain_grad]).reshape(2, -1, feature_width)
    packet = after(packet, cols)
    packet = pick(packet, core) + flip_dp(pick(packet, 1 - core).astype(BF16), 1).astype(F32)
    packet = packet.astype(BF16)
    packet = tree_sum(
        [packet.astype(F32)]
        + [flip_dp(packet, mask).astype(F32) for mask in range(2, n_dp, 2)]
    )
    packet = packet.astype(BF16)
    packet = tree_sum(
        [packet.astype(F32)]
        + [flip_fsdp(packet, mask).astype(F32) for mask in range(1, n_fsdp)]
    )
    packet = ordered(core, packet, flip_dp(packet, 1), 0).reshape(-1, feature_width)

    return (
        loss,
        grad_head,
        grad_point,
        packet[:tap_count],
        packet[tap_count],
        grad_residual,
        glu_grad.astype(BF16),
    )


def solution(mesh):
    placed = (
        P(("dp", "fsdp"), None),
        P(("dp", "fsdp"), None),
        P("dp", "fsdp", None, None),
        P("dp", "fsdp", None),
        P("dp", "fsdp", None),
        P("dp", None),
        P(),
        P(),
        P("fsdp", None),
        P(None, "fsdp"),
    )
    return jax.shard_map(
        local,
        mesh=mesh,
        in_specs=placed,
        out_specs=(
            P(),
            P("dp", "fsdp"),
            P("fsdp", "dp"),
            P(),
            P(),
            P(("dp", "fsdp"), None),
            P(("dp", "fsdp"), None),
        ),
        check_vma=False,
    )
```

```python
import functools

import jax
import jax.numpy as jnp
from jax import lax
from jax.experimental import pallas as pl
from jax.experimental.pallas import tpu as pltpu
from jax.sharding import PartitionSpec as P

F32 = jnp.float32
BF16 = jnp.bfloat16


def flip_dp(value, mask):
    count = lax.axis_size("dp")
    return lax.ppermute(value, "dp", [(i, i ^ mask) for i in range(count)])


def flip_fsdp(value, mask):
    count = lax.axis_size("fsdp")
    return lax.ppermute(value, "fsdp", [(i, i ^ mask) for i in range(count)])


def shift_fsdp(value, step):
    count = lax.axis_size("fsdp")
    return lax.ppermute(value, "fsdp", [(i, (i + step) % count) for i in range(count)])


def pick(array, index, axis=0):
    return lax.dynamic_index_in_dim(array, index, axis, keepdims=False)


def ordered(bit, own, other, axis):
    return jnp.where(
        bit == 0, jnp.stack([own, other], axis), jnp.stack([other, own], axis)
    )


def tree_sum(values):
    while len(values) > 1:
        values = [values[i] + values[i + 1] for i in range(0, len(values), 2)]
    return values[0]


def after(value, *others):
    return lax.optimization_barrier((value, *others))[0]


def gather_point(point_weight, d, activation):
    count = lax.axis_size("fsdp")
    rows, width = point_weight.shape
    core, bit1, bit2 = d & 1, (d >> 1) & 1, (d >> 2) & 1
    parts = point_weight.reshape(2, 2, 2, rows // 8, width)
    piece1 = pick(pick(parts[0], bit1), core)
    piece2 = pick(pick(parts[1], bit2), core)
    piece = jnp.stack([piece1, piece2])
    got = jnp.stack([shift_fsdp(piece, step) for step in range(1, count)], 1)
    across = [flip_dp(got[0], 2), flip_dp(got[1], 4)]
    far = [flip_dp(got, 1)] + [flip_dp(after(piece, activation), 1) for piece in across]
    return [got] + across + far


def branch_kernel(
    place, weight, act, residual, got, got1, got2, far, far1, far2, kept, out, panel, sems, keep
):
    count = panel.shape[0]
    d, f = place[0], place[1]
    core, bits = d & 1, ((d >> 1) & 1, (d >> 2) & 1)
    copies = [(weight, panel.at[f])]
    for step in range(1, count):
        shard = panel.at[lax.rem(f + count - step, count)]
        for mine, others, side in (
            (got, (got1, got2), core),
            (far, (far1, far2), 1 - core),
        ):
            for half in range(2):
                copies.append((mine.at[half, step - 1], shard.at[half, bits[half], side]))
                copies.append((others[half].at[step - 1], shard.at[half, 1 - bits[half], side]))
    copies = [
        pltpu.make_async_copy(source, target, sems.at[i])
        for i, (source, target) in enumerate(copies)
    ]
    for copy in copies:
        copy.start()
    for copy in copies:
        copy.wait()
    keeping = pltpu.make_async_copy(panel, kept, keep)
    keeping.start()
    rows, width = act.shape
    tile = 512
    whole = panel.reshape(act.shape[1], width)

    @pl.loop(0, width // tile)
    def _(step):
        lanes = pl.ds(pl.multiple_of(step * tile, tile), tile)
        total = jnp.dot(act[...], whole[:, lanes], preferred_element_type=F32)
        out[:, lanes] = (residual[:, lanes].astype(F32) + total).astype(BF16)

    keeping.wait()


def branch(point_weight, activation, residual_owned, pieces, d, f):
    count = lax.axis_size("fsdp")
    rows, width = point_weight.shape
    vmem = pl.BlockSpec(memory_space=pltpu.VMEM)
    panel, out = pl.pallas_call(
        branch_kernel,
        out_shape=(
            jax.ShapeDtypeStruct((count, 2, 2, 2, rows // 8, width), BF16),
            jax.ShapeDtypeStruct(activation.shape, BF16),
        ),
        in_specs=[pl.BlockSpec(memory_space=pltpu.SMEM), pl.BlockSpec(memory_space=pltpu.HBM)]
        + [vmem] * 2
        + [pl.BlockSpec(memory_space=pl.ANY)] * 6,
        out_specs=(pl.BlockSpec(memory_space=pltpu.HBM), vmem),
        scratch_shapes=[
            pltpu.VMEM((count, 2, 2, 2, rows // 8, width), BF16),
            pltpu.SemaphoreType.DMA((1 + 8 * (count - 1),)),
            pltpu.SemaphoreType.DMA,
        ],
        compiler_params=pltpu.CompilerParams(vmem_limit_bytes=60 << 20),
        name="branch",
    )(
        jnp.stack([d, f]),
        point_weight.reshape(2, 2, 2, rows // 8, width),
        activation,
        residual_owned,
        *pieces,
    )
    return panel.reshape(count * rows, width), out


EDGE = 16


def forward_kernel(
    sent, slots, masks, kernel, gain, glu, residual, standard, inv_std, act, padded, received, sem
):
    copy = pltpu.make_async_copy(sent, received, sem)
    copy.start()
    rows, width = standard.shape
    tap_count = masks.shape[0]
    half_taps = tap_count // 2
    loaders, both, _ = received.shape
    capacity = both // 2
    places = lax.broadcasted_iota(jnp.int32, (rows, loaders * capacity), 1)
    chosen = (slots[...] == places).astype(BF16)
    tile = 512
    tiles = [slice(i, i + tile) for i in range(0, width, tile)]
    for edge in (0, EDGE + rows):
        padded[pl.ds(edge, EDGE), :] = jnp.zeros((EDGE, width), F32)
    copy.wait()
    for lanes in tiles:
        for start, target in ((0, glu), (capacity, residual)):
            frames = received[:, start : start + capacity, lanes]
            frames = frames.reshape(loaders * capacity, tile)
            owned = jnp.dot(chosen, frames, preferred_element_type=F32)
            target[:, lanes] = owned.astype(BF16)
            if start == 0:
                padded[pl.ds(EDGE, rows), lanes] = owned

    @pl.loop(0, width // 128)
    def _(step):
        lanes = pl.ds(pl.multiple_of(step * 128, 128), 128)
        total = jnp.zeros((rows, 128), F32)
        for tap in range(tap_count):
            moved = padded[pl.ds(EDGE + tap - half_taps, rows), lanes]
            total = total + kernel[pl.ds(tap, 1), lanes] * (masks[tap] * moved)
        standard[:, lanes] = total

    mean = sum(jnp.sum(standard[:, lanes], axis=1, keepdims=True) for lanes in tiles) / width
    square = jnp.zeros((rows, 1), F32)
    for lanes in tiles:
        centred = standard[:, lanes] - mean
        square = square + jnp.sum(centred * centred, axis=1, keepdims=True)
    scale = lax.rsqrt(square / width + 1e-05)
    inv_std[...] = scale
    for lanes in tiles:
        unit = (standard[:, lanes] - mean) * scale
        standard[:, lanes] = unit
        normed = unit * gain[:, lanes]
        act[:, lanes] = (normed * jax.nn.sigmoid(normed)).astype(BF16)


def forward(received, slot_list, masks, kernel, gain):
    rows, width = slot_list.shape[0], received.shape[2]
    vmem = pl.BlockSpec(memory_space=pltpu.VMEM)
    half = jax.ShapeDtypeStruct((rows, width), BF16)
    return pl.pallas_call(
        forward_kernel,
        out_shape=(
            half,
            half,
            jax.ShapeDtypeStruct((rows, width), F32),
            jax.ShapeDtypeStruct((rows, 1), F32),
            half,
        ),
        in_specs=[pl.BlockSpec(memory_space=pltpu.HBM)] + [vmem] * 4,
        out_specs=(vmem,) * 5,
        scratch_shapes=[
            pltpu.VMEM((rows + 2 * EDGE, width), F32),
            pltpu.VMEM(received.shape, BF16),
            pltpu.SemaphoreType.DMA,
        ],
        compiler_params=pltpu.CompilerParams(vmem_limit_bytes=60 << 20),
        cost_estimate=pl.CostEstimate(
            flops=1_000_000_000, bytes_accessed=6_000_000, transcendentals=200_000
        ),
        name="forward",
    )(received, slot_list[:, None], masks, kernel, gain[None, :])


def code_kernel(count, index, norms, targets, *refs):
    logits, head = refs[:count], refs[count]
    grads, outs = refs[count + 1 : 2 * count + 1], refs[2 * count + 1 : 3 * count + 1]
    norm, target, total, held, sems = refs[3 * count + 1 :]
    rows, codes = logits[0].shape
    parts, _, tile = held.shape
    copies = [
        pltpu.make_async_copy(head.at[:, pl.ds(i * tile, tile)], held.at[i], sems.at[i])
        for i in range(parts)
    ]
    for copy in copies:
        copy.start()
    for i in range(count):
        for table, column in ((norms, norm), (targets, target)):
            line = table[pl.ds(index[i], 1), :]
            column[i] = jnp.broadcast_to(line, (rows, rows)).T
    for part in range(parts):
        lanes = slice(part * tile, (part + 1) * tile)
        columns = lax.broadcasted_iota(jnp.int32, (rows, tile), 1) + part * tile
        values = []
        for i in range(count):
            hits = (columns == target[i][:, :1].astype(jnp.int32)).astype(F32)
            value = (jnp.exp(logits[i][:, lanes] - norm[i][:, :1]) - hits).astype(BF16)
            grads[i][:, lanes] = value
            values.append(value)
        value = jnp.concatenate(values) if count > 1 else values[0]
        copies[part].wait()
        product = lax.dot_general(
            value, held[part], (((1,), (1,)), ((), ())), preferred_element_type=F32
        )
        if part:
            product = total[...] + product
        if part < parts - 1:
            total[...] = product
        else:
            for i in range(count):
                outs[i][...] = product[i * rows : (i + 1) * rows].astype(outs[i].dtype)


def code_grad(logits, index, norms, targets, head, dtype):
    count = len(logits)
    rows, codes = logits[0].shape
    width, tile = head.shape[0], 512
    vmem = pl.BlockSpec(memory_space=pltpu.VMEM)
    made = pl.pallas_call(
        functools.partial(code_kernel, count),
        out_shape=[jax.ShapeDtypeStruct((rows, codes), BF16)] * count
        + [jax.ShapeDtypeStruct((rows, width), dtype)] * count,
        in_specs=[pl.BlockSpec(memory_space=pltpu.SMEM)]
        + [vmem] * (count + 2)
        + [pl.BlockSpec(memory_space=pltpu.HBM)],
        out_specs=[vmem] * (2 * count),
        scratch_shapes=[
            pltpu.VMEM((count, rows, rows), F32),
            pltpu.VMEM((count, rows, rows), F32),
            pltpu.VMEM((count * rows, width), F32),
            pltpu.VMEM((codes // tile, width, tile), BF16),
            pltpu.SemaphoreType.DMA((codes // tile,)),
        ],
        compiler_params=pltpu.CompilerParams(vmem_limit_bytes=(10 + 4 * count) << 20),
        cost_estimate=pl.CostEstimate(
            flops=800_000_000 * count, bytes_accessed=8_000_000, transcendentals=200_000 * count
        ),
        name="code",
    )(index, norms, targets.astype(F32), *logits, head)
    return made[:count], made[count:]


def head_kernel(count, place, *refs):
    rows, grads, mine, sent = refs[:count], refs[count : 2 * count], refs[-2], refs[-1]
    core = place[0]
    pairs, height, codes = mine.shape
    tile = min(512, codes)
    for pair in range(pairs):
        side = slice(2 * pair * height, (2 * pair + 2) * height)
        turned = jnp.concatenate([block[:, side] for block in rows]).T
        for step in range(codes // tile):
            lanes = slice(step * tile, (step + 1) * tile)
            product = jnp.dot(
                turned,
                jnp.concatenate([grad[:, lanes] for grad in grads]),
                preferred_element_type=F32,
            ).astype(BF16)

            @pl.when(core == 0)
            def _():
                mine[pair, :, lanes] = product[:height]
                sent[pair, :, lanes] = product[height:]

            @pl.when(core != 0)
            def _():
                mine[pair, :, lanes] = product[height:]
                sent[pair, :, lanes] = product[:height]


def head_grad(rows, grads, core):
    n_dp = lax.axis_size("dp")
    count = len(rows)
    half = jax.ShapeDtypeStruct((n_dp // 2, rows[0].shape[1] // n_dp, grads[0].shape[1]), BF16)
    vmem = pl.BlockSpec(memory_space=pltpu.VMEM)
    return pl.pallas_call(
        functools.partial(head_kernel, count),
        out_shape=(half, half),
        in_specs=[pl.BlockSpec(memory_space=pltpu.SMEM)] + [vmem] * (2 * count),
        out_specs=(vmem, vmem),
        compiler_params=pltpu.CompilerParams(vmem_limit_bytes=20 << 20),
        cost_estimate=pl.CostEstimate(flops=1000, bytes_accessed=1000, transcendentals=0),
        name="head",
    )(core[None], *rows, *grads)


def point_kernel(count, place, cols, *refs):
    given = refs[:count]
    own, out, acts, parts, sems = refs[count:]
    d, f = place[0], place[1]
    copies = [pltpu.make_async_copy(given[i], acts.at[i], sems.at[i]) for i in range(count)]
    for copy in copies:
        copy.start()
    for copy in copies:
        copy.wait()
    blocks, _, width = out.shape
    for block in range(blocks):
        lanes = slice(block * width, (block + 1) * width)
        total = jnp.zeros(out.shape[1:], F32)
        for mask in range(count):
            total = total + jnp.dot(
                cols[d ^ mask], acts[mask, :, lanes], preferred_element_type=F32
            )
        out[f ^ block] = total.astype(BF16)
        parts[block] = total
    own[...] = parts[f]


def point_part(cols, acts, d, f):
    n_fsdp = lax.axis_size("fsdp")
    width = acts[0].shape[1] // n_fsdp
    vmem = pl.BlockSpec(memory_space=pltpu.VMEM)
    return pl.pallas_call(
        functools.partial(point_kernel, len(acts)),
        out_shape=(
            jax.ShapeDtypeStruct((cols.shape[1], width), F32),
            jax.ShapeDtypeStruct((n_fsdp, cols.shape[1], width), BF16),
        ),
        in_specs=[pl.BlockSpec(memory_space=pltpu.SMEM), vmem]
        + [pl.BlockSpec(memory_space=pltpu.HBM)] * len(acts),
        out_specs=(vmem, vmem),
        scratch_shapes=[
            pltpu.VMEM((len(acts), *acts[0].shape), BF16),
            pltpu.VMEM((n_fsdp, cols.shape[1], width), F32),
            pltpu.SemaphoreType.DMA((len(acts),)),
        ],
        compiler_params=pltpu.CompilerParams(vmem_limit_bytes=60 << 20),
        cost_estimate=pl.CostEstimate(flops=1000, bytes_accessed=1000, transcendentals=0),
        name="point",
    )(jnp.stack([d, f]), cols, *acts)


def gather_rows(own, f):
    count = lax.axis_size("fsdp")
    if count != 4:
        return [(0, own)] + [(count - step, shift_fsdp(own, step)) for step in range(1, count)]
    before = shift_fsdp(own, 1)
    after = shift_fsdp(own, -1)
    source = jnp.where(f == 2, before, jnp.where(f == 1, after, own))
    across = lax.ppermute(source, "fsdp", [(0, 2), (3, 1), (2, 3), (1, 0)])
    return [(0, own), (3, before), (1, after), (2, across)]


def scatter_rows(code_part, gathered, d, f):
    count = lax.axis_size("fsdp")

    places = [distance for distance, _ in gathered]

    def head_halves(grads):
        return head_grad([block for _, block in gathered], [grads[p] for p in places], d & 1)

    if count != 4:
        grads, outs = code_part(places, F32)
        grads, outs = dict(zip(places, grads)), dict(zip(places, outs))
        got = [shift_fsdp(outs[step].astype(BF16), step).astype(F32) for step in range(1, count)]
        return sum(got, outs[0]), join_cores(*head_halves(grads), d)
    grads = {}
    (grads[2],), (block,) = code_part([2], BF16)
    across = lax.ppermute(block, "fsdp", [(2, 0), (1, 3), (3, 2), (0, 1)])
    (grads[1], grads[3], grads[0]), (ahead, behind, own) = code_part([1, 3, 0], F32)
    across = after(across, own).astype(F32)
    ahead = (ahead + jnp.where(f == 1, across, 0.0)).astype(BF16)
    behind = (behind + jnp.where(f == 2, across, 0.0)).astype(BF16)
    got1 = shift_fsdp(ahead, 1)
    got2 = shift_fsdp(behind, -1)
    direct = jnp.where((f == 0) | (f == 3), across, 0.0)
    mine, sent = head_halves({place: after(grads[place], ahead, behind) for place in places})
    sides = join_cores(mine, sent, d)
    got1 = after(got1, *[keep for keep, _, _ in sides])
    return own + direct + got1.astype(F32) + got2.astype(F32), sides


def fold_kernel(cut, place, *refs):
    ins, outs, held, sems = refs[:4], refs[4:8], refs[8:12], refs[12]
    copies = []
    for i, (source, target) in enumerate(zip(ins, held)):
        if cut:
            width = target.shape[-1]
            source = source.at[:, :, :, :, pl.ds(i // 2 * width, width)]
        copies.append(pltpu.make_async_copy(source, target, sems.at[i]))
        copies[-1].start()
    for side in range(2):
        own, other = held[2 * side], held[2 * side + 1]
        copies[2 * side].wait()
        copies[2 * side + 1].wait()
        keep, send = outs[2 * side], outs[2 * side + 1]
        before, _, behind = own.shape[:3]
        for first in range(before):
            for last in range(behind):
                for target, half in ((keep, place[side]), (send, 1 - place[side])):
                    total = own[first, half, last].astype(F32) + other[first, half, last].astype(F32)
                    target[first, last] = total.astype(target.dtype)


def fold(sides, d, cut=False):
    ins, outs, held, left_over = [], [], [], []
    for own, other, left, bit in sides:
        place = left.index(bit)
        rows, width = own.shape[-2:]
        part = width // 2 if cut else width
        before, behind = 2**place, 2 ** (len(left) - 1 - place)
        ins += [value.reshape(before, 2, behind, rows, width) for value in (own, other)]
        held += [pltpu.VMEM((before, 2, behind, rows, part), BF16)] * 2
        outs += [jax.ShapeDtypeStruct((before, behind, rows, part), BF16)] * 2
        left_over.append([b for b in left if b != bit])
    vmem = pl.BlockSpec(memory_space=pltpu.VMEM)
    made = pl.pallas_call(
        functools.partial(fold_kernel, cut),
        out_shape=outs,
        in_specs=[pl.BlockSpec(memory_space=pltpu.SMEM)] + [pl.BlockSpec(memory_space=pl.ANY)] * 4,
        out_specs=[vmem] * 4,
        scratch_shapes=held + [pltpu.SemaphoreType.DMA((4,))],
        compiler_params=pltpu.CompilerParams(vmem_limit_bytes=16 << 20),
        cost_estimate=pl.CostEstimate(flops=1000, bytes_accessed=1000, transcendentals=0),
        name="fold",
    )(jnp.stack([(d >> side[3]) & 1 for side in sides]), *ins)
    return [(made[2 * i], made[2 * i + 1], left_over[i]) for i in range(2)]


def last_kernel(*refs):
    out = refs[4]
    width = refs[0].shape[-1]
    for side in range(2):
        total = refs[2 * side][...].astype(F32) + refs[2 * side + 1][...].astype(F32)
        out[:, side * width : (side + 1) * width] = total


def last_fold(parts):
    rows, width = parts[0].shape[-2:]
    vmem = pl.BlockSpec(memory_space=pltpu.VMEM)
    return pl.pallas_call(
        last_kernel,
        out_shape=jax.ShapeDtypeStruct((rows, 2 * width), F32),
        in_specs=[vmem] * 4,
        out_specs=vmem,
        compiler_params=pltpu.CompilerParams(vmem_limit_bytes=12 << 20),
        cost_estimate=pl.CostEstimate(flops=1000, bytes_accessed=1000, transcendentals=0),
        name="last",
    )(*[part.reshape(rows, width) for part in parts])


def halve_bits(step):
    bits = lax.axis_size("dp").bit_length() - 1
    return [list(range(1, bits))[step], list(range(bits - 1, 0, -1))[step]]


def join_cores(mine, sent, d):
    left = list(range(lax.axis_size("dp").bit_length() - 2, 0, -1))
    got = flip_dp(sent, 1)
    sides = [(mine, got, left, bit) for bit in halve_bits(0)]
    return send_on(fold(sides, d, True), 0)


def send_on(folded, step):
    return [
        (keep, flip_dp(send, 1 << bit), left)
        for (keep, send, left), bit in zip(folded, halve_bits(step))
    ]


def middle_folds(sides, d):
    bits = lax.axis_size("dp").bit_length() - 1
    for step in range(1, bits - 1):
        ready = [(*side, bit) for side, bit in zip(sides, halve_bits(step))]
        sides = send_on(fold(ready, d), step)
    return sides


def taps_kernel(
    grad, panel, standard, inv_std, gain, glu, masks, loss, packet, conv_grad, scaled, padded, *held
):
    rows, width = standard.shape
    tap_count = masks.shape[0]
    half_taps = tap_count // 2
    tile = 512
    panel_held, standard_held, glu_held, masks_held, sems = held
    copies = [
        pltpu.make_async_copy(source, target, sems.at[i])
        for i, (source, target) in enumerate(
            [(standard, standard_held)]
            + [
                (panel.at[pl.ds(i * tile, tile)], panel_held.at[pl.ds(i * tile, tile)])
                for i in range(width // tile)
            ]
            + [(glu, glu_held), (masks, masks_held)]
        )
    ]
    for copy in copies:
        copy.start()
    panel, standard, glu, masks = panel_held, standard_held, glu_held, masks_held
    copies[0].wait()
    parts = packet.shape[2] // 128
    rest = packet.shape[1] - tap_count - 1
    packet[:, pl.ds(tap_count + 1, rest), :] = jnp.full((2, rest, packet.shape[2]), loss[0, 0])
    sums = jnp.zeros((rows, 1), F32)
    dots = jnp.zeros((rows, 1), F32)
    for lanes in [slice(i, i + tile) for i in range(0, width, tile)]:
        copies[1 + lanes.start // tile].wait()
        act_grad = lax.dot_general(
            grad[...], panel[lanes, :], (((1,), (1,)), ((), ())), preferred_element_type=F32
        )
        scale = gain[:, lanes]
        unit = standard[:, lanes]
        normed = unit * scale
        sig = jax.nn.sigmoid(normed)
        normed_grad = act_grad * sig * (1.0 + normed * (1.0 - sig))
        gain_grad = jnp.sum(normed_grad * unit, axis=0, keepdims=True)
        for first in range(0, tile, 128):
            half, place = divmod(lanes.start + first, packet.shape[2])
            packet[half, pl.ds(tap_count, 1), place : place + 128] = gain_grad[
                :, first : first + 128
            ]
        part = normed_grad * scale
        scaled[:, lanes] = part
        sums = sums + jnp.sum(part, axis=1, keepdims=True)
        dots = dots + jnp.sum(part * unit, axis=1, keepdims=True)
    for copy in copies[-2:]:
        copy.wait()
    sums, dots, scale = sums / width, dots / width, inv_std[...]
    for edge in (0, EDGE + rows):
        conv_grad[pl.ds(edge, EDGE), :] = jnp.zeros((EDGE, width), F32)
        padded[pl.ds(edge, EDGE), :] = jnp.zeros((EDGE, width), F32)
    for lanes in [slice(i, i + tile) for i in range(0, width, tile)]:
        conv_grad[pl.ds(EDGE, rows), lanes] = scale * (
            scaled[:, lanes] - sums - standard[:, lanes] * dots
        )
        padded[pl.ds(EDGE, rows), lanes] = glu[:, lanes].astype(F32)

    @pl.loop(0, width // 128)
    def _(step):
        lanes = pl.ds(pl.multiple_of(step * 128, 128), 128)
        place = pl.ds(pl.multiple_of(lax.rem(step, parts) * 128, 128), 128)
        value = conv_grad[pl.ds(EDGE, rows), lanes]
        for tap in range(tap_count):
            moved = padded[pl.ds(EDGE + tap - half_taps, rows), lanes]
            packet[step // parts, pl.ds(tap, 1), place] = jnp.sum(
                value * (masks[tap] * moved), axis=0, keepdims=True
            )


def taps(grad, panel, standard, inv_std, gain, glu, masks, loss):
    rows, width = standard.shape
    whole = pl.BlockSpec(memory_space=pltpu.HBM)
    vmem = pl.BlockSpec(memory_space=pltpu.VMEM)
    return pl.pallas_call(
        taps_kernel,
        out_shape=(
            jax.ShapeDtypeStruct((2, (masks.shape[0] + 9) // 8 * 8, width // 2), F32),
            jax.ShapeDtypeStruct((rows + 2 * EDGE, width), F32),
        ),
        in_specs=[vmem, whole, whole, vmem, vmem, whole, whole]
        + [pl.BlockSpec(memory_space=pltpu.SMEM)],
        out_specs=(vmem, vmem),
        scratch_shapes=[
            pltpu.VMEM((rows, width), F32),
            pltpu.VMEM((rows + 2 * EDGE, width), F32),
            pltpu.VMEM(panel.shape, BF16),
            pltpu.VMEM(standard.shape, F32),
            pltpu.VMEM(glu.shape, BF16),
            pltpu.VMEM(masks.shape, F32),
            pltpu.SemaphoreType.DMA((3 + width // 512,)),
        ],
        compiler_params=pltpu.CompilerParams(vmem_limit_bytes=60 << 20),
        cost_estimate=pl.CostEstimate(flops=1000, bytes_accessed=1000, transcendentals=0),
        name="taps",
    )(grad, panel, standard, inv_std, gain[None, :], glu, masks, loss)


def spread_kernel(conv_grad, kernel, masks, out):
    rows, width = out.shape
    tap_count = masks.shape[0]
    half_taps = tap_count // 2

    @pl.loop(0, width // 128)
    def _(step):
        lanes = pl.ds(pl.multiple_of(step * 128, 128), 128)
        total = jnp.zeros((rows, 128), F32)
        for tap in range(tap_count):
            moved = conv_grad[pl.ds(EDGE + half_taps - tap, rows), lanes]
            total = total + kernel[pl.ds(tap, 1), lanes] * (
                masks[tap_count - 1 - tap] * moved
            )
        out[:, lanes] = total.astype(BF16)


def spread(conv_grad, kernel, masks):
    vmem = pl.BlockSpec(memory_space=pltpu.VMEM)
    return pl.pallas_call(
        spread_kernel,
        out_shape=jax.ShapeDtypeStruct((conv_grad.shape[0] - 2 * EDGE, kernel.shape[1]), BF16),
        in_specs=[vmem] * 3,
        out_specs=vmem,
        compiler_params=pltpu.CompilerParams(vmem_limit_bytes=12 << 20),
        cost_estimate=pl.CostEstimate(flops=6_000_000_000, bytes_accessed=3_000_000, transcendentals=0),
        name="spread",
    )(conv_grad, kernel, masks)


def local(
    glu_frames,
    residual_frames,
    send_rows,
    recv_slot,
    segment_ids,
    code_targets,
    conv_kernel,
    norm_gain,
    point_weight,
    code_head,
):
    n_dp, n_fsdp = lax.axis_size("dp"), lax.axis_size("fsdp")
    d, f = lax.axis_index("dp"), lax.axis_index("fsdp")
    feature_width = glu_frames.shape[1]
    tap_count = conv_kernel.shape[0]
    half_taps = tap_count // 2
    slot_list = recv_slot[0, 0]
    row_count = slot_list.shape[0]
    picked_rows = send_rows[0, 0]

    capacity = picked_rows.shape[1]
    sent = jnp.concatenate([glu_frames[picked_rows], residual_frames[picked_rows]], axis=1)
    received = lax.all_to_all(sent, "dp", split_axis=0, concat_axis=0, tiled=True)
    segments = segment_ids[0, 0]
    seg_pad = jnp.pad(segments, (half_taps, half_taps), constant_values=-1)
    masks = jnp.stack(
        [seg_pad[offset : offset + row_count] == segments for offset in range(tap_count)]
    )
    masks = jnp.broadcast_to(masks.astype(F32)[:, :, None], (*masks.shape, 128))
    glu_owned, residual_owned, standard, inv_std, activation = forward(
        received, slot_list, masks, conv_kernel, norm_gain
    )

    pieces = gather_point(point_weight, d, activation)
    full_panel, residual_new = branch(
        point_weight, activation, residual_owned, pieces, d, f
    )

    code_local = code_head.shape[1]
    targets = code_targets[0].reshape(n_fsdp, row_count) - f * code_local
    columns = lax.broadcasted_iota(jnp.int32, (1, code_local), 1)
    gathered = gather_rows(residual_new, f)
    logits, hits, stats = {}, {}, {}
    act_own = after(activation, residual_new)
    acts = {mask: flip_dp(act_own, mask) if mask else act_own for mask in range(0, n_dp, 2)}
    acts.update({mask + 1: flip_dp(act, 1) for mask, act in list(acts.items())})
    gathered[-1] = (gathered[-1][0], after(gathered[-1][1], *acts.values()))
    for distance, block in gathered:
        logits[distance] = jnp.dot(block, code_head, preferred_element_type=F32)
        hits[distance] = pick(targets, (f + distance) % n_fsdp)[:, None] == columns
        top = jnp.max(logits[distance], axis=1)
        total = jnp.sum(jnp.exp(logits[distance] - top[:, None]), axis=1)
        chosen = jnp.sum(jnp.where(hits[distance], logits[distance], 0.0), axis=1)
        stats[distance] = jnp.stack([top, total, chosen])
    places = jnp.arange(n_fsdp)[:, None, None]
    table = tree_sum(
        [
            jnp.where(places == (f + distance) % n_fsdp, stats[distance], 0.0)
            for distance, _ in gathered
        ]
    )
    tables = [table] + [flip_fsdp(table, mask) for mask in range(1, n_fsdp)]
    tops = tables[0][:, 0]
    for other in tables[1:]:
        tops = jnp.maximum(tops, other[:, 0])
    sums = tree_sum([t[:, 1] * jnp.exp(t[:, 0] - tops) for t in tables])
    log_norm = tops + jnp.log(sums)
    loss_part = jnp.sum(log_norm - tree_sum([t[:, 2] for t in tables]))

    def code_part(distances, dtype):
        index = jnp.stack([(f + distance) % n_fsdp for distance in distances])
        return code_grad(
            [logits[distance] for distance in distances],
            index,
            log_norm,
            targets,
            code_head,
            dtype,
        )

    grad_residual, sides = scatter_rows(code_part, gathered, d, f)
    grad_residual, turned = lax.optimization_barrier(
        (grad_residual.astype(BF16), grad_residual.astype(BF16).T)
    )

    part_width = feature_width // n_dp
    cols = lax.all_to_all(
        turned.reshape(n_dp, part_width, row_count),
        "dp",
        split_axis=0,
        concat_axis=0,
        tiled=True,
    )
    packet, conv_grad = taps(
        grad_residual,
        full_panel,
        standard,
        inv_std,
        norm_gain,
        glu_owned,
        masks,
        loss_part.reshape(1, 1),
    )

    core = d & 1
    packet = after(packet, cols)
    packet = pick(packet, core) + flip_dp(pick(packet, 1 - core).astype(BF16), 1).astype(F32)
    packet = packet.astype(BF16)
    cols = after(cols, packet)
    point_own, point_sent = point_part(cols, [acts[mask] for mask in range(n_dp)], d, f)
    sides = [(keep, after(other, point_sent), left) for keep, other, left in sides]
    sides = middle_folds(sides, d)
    ready = [keep for keep, _, _ in sides]
    others = [after(flip_dp(packet, mask), *ready) for mask in range(2, n_dp, 2)]
    packet = tree_sum([packet.astype(F32)] + [other.astype(F32) for other in others])
    packet = packet.astype(BF16)
    grad_point = tree_sum(
        [point_own]
        + [flip_fsdp(point_sent[mask], mask).astype(F32) for mask in range(1, n_fsdp)]
    ).T
    grad_glu = spread(after(conv_grad, packet), conv_kernel, masks)
    grad_head = last_fold([after(part, packet) for keep, other, _ in sides for part in (keep, other)])
    others = [
        after(flip_fsdp(packet, mask), grad_glu, grad_head) for mask in range(1, n_fsdp)
    ]
    packet = tree_sum([packet.astype(F32)] + [other.astype(F32) for other in others])
    packet = ordered(core, packet, flip_dp(packet, 1), 1).reshape(-1, feature_width)
    loss = packet[tap_count + 1, 0] / (row_count * n_dp * n_fsdp * n_fsdp)
    return (
        loss,
        grad_head,
        grad_point,
        packet[:tap_count],
        packet[tap_count],
        grad_residual,
        grad_glu,
    )


def solution(mesh):
    placed = (
        P(("dp", "fsdp"), None),
        P(("dp", "fsdp"), None),
        P("dp", "fsdp", None, None),
        P("dp", "fsdp", None),
        P("dp", "fsdp", None),
        P("dp", None),
        P(),
        P(),
        P("fsdp", None),
        P(None, "fsdp"),
    )
    return jax.shard_map(
        local,
        mesh=mesh,
        in_specs=placed,
        out_specs=(
            P(),
            P("dp", "fsdp"),
            P("fsdp", "dp"),
            P(),
            P(),
            P(("dp", "fsdp"), None),
            P(("dp", "fsdp"), None),
        ),
        check_vma=False,
    )
```

```python
import functools

import jax
import jax.numpy as jnp
from jax import lax
from jax.experimental import pallas as pl
from jax.experimental.pallas import tpu as pltpu
from jax.sharding import PartitionSpec as P

F32 = jnp.float32
BF16 = jnp.bfloat16


def flip_dp(value, mask):
    count = lax.axis_size("dp")
    return lax.ppermute(value, "dp", [(i, i ^ mask) for i in range(count)])


def flip_fsdp(value, mask):
    count = lax.axis_size("fsdp")
    return lax.ppermute(value, "fsdp", [(i, i ^ mask) for i in range(count)])


def shift_fsdp(value, step):
    count = lax.axis_size("fsdp")
    return lax.ppermute(value, "fsdp", [(i, (i + step) % count) for i in range(count)])


def pick(array, index, axis=0):
    return lax.dynamic_index_in_dim(array, index, axis, keepdims=False)


def ordered(bit, own, other, axis):
    return jnp.where(
        bit == 0, jnp.stack([own, other], axis), jnp.stack([other, own], axis)
    )


def tree_sum(values):
    while len(values) > 1:
        values = [values[i] + values[i + 1] for i in range(0, len(values), 2)]
    return values[0]


def after(value, *others):
    return lax.optimization_barrier((value, *others))[0]


def gather_point(point_weight, d, activation):
    count = lax.axis_size("fsdp")
    rows, width = point_weight.shape
    core, bit1, bit2 = d & 1, (d >> 1) & 1, (d >> 2) & 1
    parts = point_weight.reshape(2, 2, 2, rows // 8, width)
    piece1 = pick(pick(parts[0], bit1), core)
    piece2 = pick(pick(parts[1], bit2), core)
    piece = jnp.stack([piece1, piece2])
    got = jnp.stack([shift_fsdp(piece, step) for step in range(1, count)], 1)
    across = [flip_dp(got[0], 2), flip_dp(got[1], 4)]
    far = [flip_dp(got, 1)] + [flip_dp(after(piece, activation), 1) for piece in across]
    return [got] + across + far


def branch_kernel(
    place, weight, act, residual, got, got1, got2, far, far1, far2, kept, out, panel, sems, keep
):
    count = panel.shape[0]
    d, f = place[0], place[1]
    core, bits = d & 1, ((d >> 1) & 1, (d >> 2) & 1)
    copies = [(weight, panel.at[f])]
    for step in range(1, count):
        shard = panel.at[lax.rem(f + count - step, count)]
        for mine, others, side in (
            (got, (got1, got2), core),
            (far, (far1, far2), 1 - core),
        ):
            for half in range(2):
                copies.append((mine.at[half, step - 1], shard.at[half, bits[half], side]))
                copies.append((others[half].at[step - 1], shard.at[half, 1 - bits[half], side]))
    copies = [
        pltpu.make_async_copy(source, target, sems.at[i])
        for i, (source, target) in enumerate(copies)
    ]
    for copy in copies:
        copy.start()
    for copy in copies:
        copy.wait()
    keeping = pltpu.make_async_copy(panel, kept, keep)
    keeping.start()
    rows, width = act.shape
    tile = 512
    whole = panel.reshape(act.shape[1], width)

    @pl.loop(0, width // tile)
    def _(step):
        lanes = pl.ds(pl.multiple_of(step * tile, tile), tile)
        total = jnp.dot(act[...], whole[:, lanes], preferred_element_type=F32)
        out[:, lanes] = (residual[:, lanes].astype(F32) + total).astype(BF16)

    keeping.wait()


def branch(point_weight, activation, residual_owned, pieces, d, f):
    count = lax.axis_size("fsdp")
    rows, width = point_weight.shape
    vmem = pl.BlockSpec(memory_space=pltpu.VMEM)
    panel, out = pl.pallas_call(
        branch_kernel,
        out_shape=(
            jax.ShapeDtypeStruct((count, 2, 2, 2, rows // 8, width), BF16),
            jax.ShapeDtypeStruct(activation.shape, BF16),
        ),
        in_specs=[pl.BlockSpec(memory_space=pltpu.SMEM), pl.BlockSpec(memory_space=pltpu.HBM)]
        + [vmem] * 2
        + [pl.BlockSpec(memory_space=pl.ANY)] * 6,
        out_specs=(pl.BlockSpec(memory_space=pltpu.HBM), vmem),
        scratch_shapes=[
            pltpu.VMEM((count, 2, 2, 2, rows // 8, width), BF16),
            pltpu.SemaphoreType.DMA((1 + 8 * (count - 1),)),
            pltpu.SemaphoreType.DMA,
        ],
        compiler_params=pltpu.CompilerParams(vmem_limit_bytes=60 << 20),
        name="branch",
    )(
        jnp.stack([d, f]),
        point_weight.reshape(2, 2, 2, rows // 8, width),
        activation,
        residual_owned,
        *pieces,
    )
    return panel.reshape(count * rows, width), out


EDGE = 16


def forward_kernel(
    sent, slots, masks, kernel, gain, glu, residual, standard, inv_std, act, padded, received, sem
):
    copy = pltpu.make_async_copy(sent, received, sem)
    copy.start()
    rows, width = standard.shape
    tap_count = masks.shape[0]
    half_taps = tap_count // 2
    loaders, both, _ = received.shape
    capacity = both // 2
    places = lax.broadcasted_iota(jnp.int32, (rows, loaders * capacity), 1)
    chosen = (slots[...] == places).astype(BF16)
    tile = 512
    tiles = [slice(i, i + tile) for i in range(0, width, tile)]
    for edge in (0, EDGE + rows):
        padded[pl.ds(edge, EDGE), :] = jnp.zeros((EDGE, width), F32)
    copy.wait()
    for lanes in tiles:
        for start, target in ((0, glu), (capacity, residual)):
            frames = received[:, start : start + capacity, lanes]
            frames = frames.reshape(loaders * capacity, tile)
            owned = jnp.dot(chosen, frames, preferred_element_type=F32)
            target[:, lanes] = owned.astype(BF16)
            if start == 0:
                padded[pl.ds(EDGE, rows), lanes] = owned

    @pl.loop(0, width // 128)
    def _(step):
        lanes = pl.ds(pl.multiple_of(step * 128, 128), 128)
        total = jnp.zeros((rows, 128), F32)
        for tap in range(tap_count):
            moved = padded[pl.ds(EDGE + tap - half_taps, rows), lanes]
            total = total + kernel[pl.ds(tap, 1), lanes] * (masks[tap] * moved)
        standard[:, lanes] = total

    mean = sum(jnp.sum(standard[:, lanes], axis=1, keepdims=True) for lanes in tiles) / width
    square = jnp.zeros((rows, 1), F32)
    for lanes in tiles:
        centred = standard[:, lanes] - mean
        square = square + jnp.sum(centred * centred, axis=1, keepdims=True)
    scale = lax.rsqrt(square / width + 1e-05)
    inv_std[...] = scale
    for lanes in tiles:
        unit = (standard[:, lanes] - mean) * scale
        standard[:, lanes] = unit
        normed = unit * gain[:, lanes]
        act[:, lanes] = (normed * jax.nn.sigmoid(normed)).astype(BF16)


def forward(received, slot_list, masks, kernel, gain):
    rows, width = slot_list.shape[0], received.shape[2]
    vmem = pl.BlockSpec(memory_space=pltpu.VMEM)
    half = jax.ShapeDtypeStruct((rows, width), BF16)
    return pl.pallas_call(
        forward_kernel,
        out_shape=(
            half,
            half,
            jax.ShapeDtypeStruct((rows, width), F32),
            jax.ShapeDtypeStruct((rows, 1), F32),
            half,
        ),
        in_specs=[pl.BlockSpec(memory_space=pltpu.HBM)] + [vmem] * 4,
        out_specs=(vmem,) * 5,
        scratch_shapes=[
            pltpu.VMEM((rows + 2 * EDGE, width), F32),
            pltpu.VMEM(received.shape, BF16),
            pltpu.SemaphoreType.DMA,
        ],
        compiler_params=pltpu.CompilerParams(vmem_limit_bytes=60 << 20),
        cost_estimate=pl.CostEstimate(
            flops=1_000_000_000, bytes_accessed=6_000_000, transcendentals=200_000
        ),
        name="forward",
    )(received, slot_list[:, None], masks, kernel, gain[None, :])


def code_kernel(count, index, norms, targets, *refs):
    logits, head = refs[:count], refs[count]
    grads, outs = refs[count + 1 : 2 * count + 1], refs[2 * count + 1 : 3 * count + 1]
    norm, target, total, held, sems = refs[3 * count + 1 :]
    rows, codes = logits[0].shape
    parts, _, tile = held.shape
    copies = [
        pltpu.make_async_copy(head.at[:, pl.ds(i * tile, tile)], held.at[i], sems.at[i])
        for i in range(parts)
    ]
    for copy in copies:
        copy.start()
    for i in range(count):
        for table, column in ((norms, norm), (targets, target)):
            line = table[pl.ds(index[i], 1), :]
            column[i] = jnp.broadcast_to(line, (rows, rows)).T
    for part in range(parts):
        lanes = slice(part * tile, (part + 1) * tile)
        columns = lax.broadcasted_iota(jnp.int32, (rows, tile), 1) + part * tile
        values = []
        for i in range(count):
            hits = (columns == target[i][:, :1].astype(jnp.int32)).astype(F32)
            value = (jnp.exp(logits[i][:, lanes] - norm[i][:, :1]) - hits).astype(BF16)
            grads[i][:, lanes] = value
            values.append(value)
        value = jnp.concatenate(values) if count > 1 else values[0]
        copies[part].wait()
        product = lax.dot_general(
            value, held[part], (((1,), (1,)), ((), ())), preferred_element_type=F32
        )
        if part:
            product = total[...] + product
        if part < parts - 1:
            total[...] = product
        else:
            for i in range(count):
                outs[i][...] = product[i * rows : (i + 1) * rows].astype(outs[i].dtype)


def code_grad(logits, index, norms, targets, head, dtype):
    count = len(logits)
    rows, codes = logits[0].shape
    width, tile = head.shape[0], 512
    vmem = pl.BlockSpec(memory_space=pltpu.VMEM)
    made = pl.pallas_call(
        functools.partial(code_kernel, count),
        out_shape=[jax.ShapeDtypeStruct((rows, codes), BF16)] * count
        + [jax.ShapeDtypeStruct((rows, width), dtype)] * count,
        in_specs=[pl.BlockSpec(memory_space=pltpu.SMEM)]
        + [vmem] * (count + 2)
        + [pl.BlockSpec(memory_space=pltpu.HBM)],
        out_specs=[vmem] * (2 * count),
        scratch_shapes=[
            pltpu.VMEM((count, rows, rows), F32),
            pltpu.VMEM((count, rows, rows), F32),
            pltpu.VMEM((count * rows, width), F32),
            pltpu.VMEM((codes // tile, width, tile), BF16),
            pltpu.SemaphoreType.DMA((codes // tile,)),
        ],
        compiler_params=pltpu.CompilerParams(vmem_limit_bytes=(10 + 4 * count) << 20),
        cost_estimate=pl.CostEstimate(
            flops=800_000_000 * count, bytes_accessed=8_000_000, transcendentals=200_000 * count
        ),
        name="code",
    )(index, norms, targets.astype(F32), *logits, head)
    return made[:count], made[count:]


def point_kernel(count, place, cols, *refs):
    given = refs[:count]
    own, outs = refs[count], refs[count + 1 : -3]
    acts, parts, sems = refs[-3:]
    d, f = place[0], place[1]
    copies = [pltpu.make_async_copy(given[i], acts.at[i], sems.at[i]) for i in range(count)]
    for copy in copies:
        copy.start()
    for copy in copies:
        copy.wait()
    blocks, _, width = parts.shape
    for block in range(blocks):
        lanes = slice(block * width, (block + 1) * width)
        total = jnp.zeros(own.shape, F32)
        for mask in range(count):
            total = total + jnp.dot(
                cols[d ^ mask], acts[mask, :, lanes], preferred_element_type=F32
            )
        parts[block] = total
    own[...] = parts[f]
    for i, out in enumerate(outs):
        out[...] = parts[f ^ (i + 1)].astype(BF16)


def point_part(cols, acts, d, f):
    n_fsdp = lax.axis_size("fsdp")
    width = acts[0].shape[1] // n_fsdp
    vmem = pl.BlockSpec(memory_space=pltpu.VMEM)
    return pl.pallas_call(
        functools.partial(point_kernel, len(acts)),
        out_shape=[jax.ShapeDtypeStruct((cols.shape[1], width), F32)]
        + [jax.ShapeDtypeStruct((cols.shape[1], width), BF16)] * (n_fsdp - 1),
        in_specs=[pl.BlockSpec(memory_space=pltpu.SMEM), vmem]
        + [pl.BlockSpec(memory_space=pltpu.HBM)] * len(acts),
        out_specs=[vmem] * n_fsdp,
        scratch_shapes=[
            pltpu.VMEM((len(acts), *acts[0].shape), BF16),
            pltpu.VMEM((n_fsdp, cols.shape[1], width), F32),
            pltpu.SemaphoreType.DMA((len(acts),)),
        ],
        compiler_params=pltpu.CompilerParams(vmem_limit_bytes=60 << 20),
        cost_estimate=pl.CostEstimate(flops=1000, bytes_accessed=1000, transcendentals=0),
        name="point",
    )(jnp.stack([d, f]), cols, *acts)


def gather_rows(own, f):
    count = lax.axis_size("fsdp")
    if count != 4:
        return [(0, own)] + [(count - step, shift_fsdp(own, step)) for step in range(1, count)]
    before = shift_fsdp(own, 1)
    after = shift_fsdp(own, -1)
    source = jnp.where(f == 2, before, jnp.where(f == 1, after, own))
    across = lax.ppermute(source, "fsdp", [(0, 2), (3, 1), (2, 3), (1, 0)])
    return [(0, own), (3, before), (1, after), (2, across)]


def scatter_rows(code_part, gathered, d, f):
    count = lax.axis_size("fsdp")

    places = [distance for distance, _ in gathered]

    def head_grad(grads):
        return lax.dot_general(
            jnp.concatenate([block for _, block in gathered]),
            jnp.concatenate([grads[place] for place in places]),
            (((0,), (0,)), ((), ())),
            preferred_element_type=F32,
        ).astype(BF16)

    if count != 4:
        grads, outs = code_part(places, F32)
        grads, outs = dict(zip(places, grads)), dict(zip(places, outs))
        got = [shift_fsdp(outs[step].astype(BF16), step).astype(F32) for step in range(1, count)]
        return sum(got, outs[0]), join_cores(head_grad(grads), d)
    grads = {}
    (grads[2],), (block,) = code_part([2], BF16)
    across = lax.ppermute(block, "fsdp", [(2, 0), (1, 3), (3, 2), (0, 1)])
    (grads[1], grads[3], grads[0]), (ahead, behind, own) = code_part([1, 3, 0], F32)
    across = after(across, own).astype(F32)
    ahead = (ahead + jnp.where(f == 1, across, 0.0)).astype(BF16)
    behind = (behind + jnp.where(f == 2, across, 0.0)).astype(BF16)
    got1 = shift_fsdp(ahead, 1)
    got2 = shift_fsdp(behind, -1)
    direct = jnp.where((f == 0) | (f == 3), across, 0.0)
    head = head_grad({place: after(grads[place], ahead, behind) for place in places})
    sides = join_cores(head, d)
    got1 = after(got1, *[keep for keep, _, _ in sides])
    return own + direct + got1.astype(F32) + got2.astype(F32), sides


def fold_kernel(cut, place, *refs):
    ins, outs, held, sems = refs[:4], refs[4:8], refs[8:12], refs[12]
    copies = []
    for i, (source, target) in enumerate(zip(ins, held)):
        if cut:
            width = target.shape[-1]
            lanes = pl.ds(i // 2 * width, width)
            if i % 2:
                source = source.at[:, :, :, :, lanes]
            else:
                source = source.at[:, :, :, place[2], :, lanes]
        copies.append(pltpu.make_async_copy(source, target, sems.at[i]))
        copies[-1].start()
    for side in range(2):
        own, other = held[2 * side], held[2 * side + 1]
        copies[2 * side].wait()
        copies[2 * side + 1].wait()
        keep, send = outs[2 * side], outs[2 * side + 1]
        before, _, behind = own.shape[:3]
        for first in range(before):
            for last in range(behind):
                for target, half in ((keep, place[side]), (send, 1 - place[side])):
                    total = own[first, half, last].astype(F32) + other[first, half, last].astype(F32)
                    target[first, last] = total.astype(target.dtype)


def fold(sides, d, cut=False):
    ins, outs, held, left_over = [], [], [], []
    for own, other, left, bit in sides:
        place = left.index(bit)
        rows, width = other.shape[-2:]
        part = width // 2 if cut else width
        before, behind = 2**place, 2 ** (len(left) - 1 - place)
        cores = (2,) if cut else ()
        ins.append(own.reshape(before, 2, behind, *cores, rows, width))
        ins.append(other.reshape(before, 2, behind, rows, width))
        held += [pltpu.VMEM((before, 2, behind, rows, part), BF16)] * 2
        outs += [jax.ShapeDtypeStruct((before, behind, rows, part), BF16)] * 2
        left_over.append([b for b in left if b != bit])
    vmem = pl.BlockSpec(memory_space=pltpu.VMEM)
    made = pl.pallas_call(
        functools.partial(fold_kernel, cut),
        out_shape=outs,
        in_specs=[pl.BlockSpec(memory_space=pltpu.SMEM)] + [pl.BlockSpec(memory_space=pl.ANY)] * 4,
        out_specs=[vmem] * 4,
        scratch_shapes=held + [pltpu.SemaphoreType.DMA((4,))],
        compiler_params=pltpu.CompilerParams(vmem_limit_bytes=16 << 20),
        cost_estimate=pl.CostEstimate(flops=1000, bytes_accessed=1000, transcendentals=0),
        name="fold",
    )(jnp.stack([(d >> side[3]) & 1 for side in sides] + [d & 1]), *ins)
    return [(made[2 * i], made[2 * i + 1], left_over[i]) for i in range(2)]


def last_kernel(*refs):
    out = refs[4]
    width = refs[0].shape[-1]
    for side in range(2):
        total = refs[2 * side][...].astype(F32) + refs[2 * side + 1][...].astype(F32)
        out[:, side * width : (side + 1) * width] = total


def last_fold(parts):
    rows, width = parts[0].shape[-2:]
    vmem = pl.BlockSpec(memory_space=pltpu.VMEM)
    return pl.pallas_call(
        last_kernel,
        out_shape=jax.ShapeDtypeStruct((rows, 2 * width), F32),
        in_specs=[vmem] * 4,
        out_specs=vmem,
        compiler_params=pltpu.CompilerParams(vmem_limit_bytes=12 << 20),
        cost_estimate=pl.CostEstimate(flops=1000, bytes_accessed=1000, transcendentals=0),
        name="last",
    )(*[part.reshape(rows, width) for part in parts])


def halve_bits(step):
    bits = lax.axis_size("dp").bit_length() - 1
    return [list(range(1, bits))[step], list(range(bits - 1, 0, -1))[step]]


def join_cores(head, d):
    count = lax.axis_size("dp")
    left = list(range(count.bit_length() - 2, 0, -1))
    cut = head.reshape(count // 2, 2, head.shape[0] // count, head.shape[1])
    got = flip_dp(pick(cut, 1 - (d & 1), 1), 1)
    sides = [(cut, got, left, bit) for bit in halve_bits(0)]
    return send_on(fold(sides, d, True), 0)


def send_on(folded, step):
    return [
        (keep, flip_dp(send, 1 << bit), left)
        for (keep, send, left), bit in zip(folded, halve_bits(step))
    ]


def middle_folds(sides, d):
    bits = lax.axis_size("dp").bit_length() - 1
    for step in range(1, bits - 1):
        ready = [(*side, bit) for side, bit in zip(sides, halve_bits(step))]
        sides = send_on(fold(ready, d), step)
    return sides


def taps_kernel(
    grad, panel, standard, inv_std, gain, glu, masks, loss, place, mine, sent, conv_grad, scaled, padded, packet, *held
):
    rows, width = standard.shape
    tap_count = masks.shape[0]
    half_taps = tap_count // 2
    tile = 512
    panel_held, standard_held, glu_held, masks_held, sems = held
    copies = [
        pltpu.make_async_copy(source, target, sems.at[i])
        for i, (source, target) in enumerate(
            [(standard, standard_held)]
            + [
                (panel.at[pl.ds(i * tile, tile)], panel_held.at[pl.ds(i * tile, tile)])
                for i in range(width // tile)
            ]
            + [(glu, glu_held), (masks, masks_held)]
        )
    ]
    for copy in copies:
        copy.start()
    panel, standard, glu, masks = panel_held, standard_held, glu_held, masks_held
    copies[0].wait()
    parts = packet.shape[2] // 128
    rest = packet.shape[1] - tap_count - 1
    packet[:, pl.ds(tap_count + 1, rest), :] = jnp.full((2, rest, packet.shape[2]), loss[0, 0])
    sums = jnp.zeros((rows, 1), F32)
    dots = jnp.zeros((rows, 1), F32)
    for lanes in [slice(i, i + tile) for i in range(0, width, tile)]:
        copies[1 + lanes.start // tile].wait()
        act_grad = lax.dot_general(
            grad[...], panel[lanes, :], (((1,), (1,)), ((), ())), preferred_element_type=F32
        )
        scale = gain[:, lanes]
        unit = standard[:, lanes]
        normed = unit * scale
        sig = jax.nn.sigmoid(normed)
        normed_grad = act_grad * sig * (1.0 + normed * (1.0 - sig))
        gain_grad = jnp.sum(normed_grad * unit, axis=0, keepdims=True)
        for first in range(0, tile, 128):
            half, first_lane = divmod(lanes.start + first, packet.shape[2])
            packet[half, pl.ds(tap_count, 1), first_lane : first_lane + 128] = gain_grad[
                :, first : first + 128
            ]
        part = normed_grad * scale
        scaled[:, lanes] = part
        sums = sums + jnp.sum(part, axis=1, keepdims=True)
        dots = dots + jnp.sum(part * unit, axis=1, keepdims=True)
    for copy in copies[-2:]:
        copy.wait()
    sums, dots, scale = sums / width, dots / width, inv_std[...]
    for edge in (0, EDGE + rows):
        conv_grad[pl.ds(edge, EDGE), :] = jnp.zeros((EDGE, width), F32)
        padded[pl.ds(edge, EDGE), :] = jnp.zeros((EDGE, width), F32)
    for lanes in [slice(i, i + tile) for i in range(0, width, tile)]:
        conv_grad[pl.ds(EDGE, rows), lanes] = scale * (
            scaled[:, lanes] - sums - standard[:, lanes] * dots
        )
        padded[pl.ds(EDGE, rows), lanes] = glu[:, lanes].astype(F32)

    @pl.loop(0, width // 128)
    def _(step):
        lanes = pl.ds(pl.multiple_of(step * 128, 128), 128)
        there = pl.ds(pl.multiple_of(lax.rem(step, parts) * 128, 128), 128)
        value = conv_grad[pl.ds(EDGE, rows), lanes]
        for tap in range(tap_count):
            moved = padded[pl.ds(EDGE + tap - half_taps, rows), lanes]
            packet[step // parts, pl.ds(tap, 1), there] = jnp.sum(
                value * (masks[tap] * moved), axis=0, keepdims=True
            )

    mine[...] = packet[place[0]]
    sent[...] = packet[1 - place[0]].astype(BF16)


def taps(grad, panel, standard, inv_std, gain, glu, masks, loss, core):
    rows, width = standard.shape
    whole = pl.BlockSpec(memory_space=pltpu.HBM)
    half = ((masks.shape[0] + 9) // 8 * 8, width // 2)
    vmem = pl.BlockSpec(memory_space=pltpu.VMEM)
    return pl.pallas_call(
        taps_kernel,
        out_shape=(
            jax.ShapeDtypeStruct(half, F32),
            jax.ShapeDtypeStruct(half, BF16),
            jax.ShapeDtypeStruct((rows + 2 * EDGE, width), F32),
        ),
        in_specs=[vmem, whole, whole, vmem, vmem, whole, whole]
        + [pl.BlockSpec(memory_space=pltpu.SMEM)] * 2,
        out_specs=(vmem,) * 3,
        scratch_shapes=[
            pltpu.VMEM((rows, width), F32),
            pltpu.VMEM((rows + 2 * EDGE, width), F32),
            pltpu.VMEM((2, *half), F32),
            pltpu.VMEM(panel.shape, BF16),
            pltpu.VMEM(standard.shape, F32),
            pltpu.VMEM(glu.shape, BF16),
            pltpu.VMEM(masks.shape, F32),
            pltpu.SemaphoreType.DMA((3 + width // 512,)),
        ],
        compiler_params=pltpu.CompilerParams(vmem_limit_bytes=60 << 20),
        cost_estimate=pl.CostEstimate(flops=1000, bytes_accessed=1000, transcendentals=0),
        name="taps",
    )(grad, panel, standard, inv_std, gain[None, :], glu, masks, loss, core[None])


def spread_kernel(conv_grad, kernel, masks, out):
    rows, width = out.shape
    tap_count = masks.shape[0]
    half_taps = tap_count // 2

    @pl.loop(0, width // 128)
    def _(step):
        lanes = pl.ds(pl.multiple_of(step * 128, 128), 128)
        total = jnp.zeros((rows, 128), F32)
        for tap in range(tap_count):
            moved = conv_grad[pl.ds(EDGE + half_taps - tap, rows), lanes]
            total = total + kernel[pl.ds(tap, 1), lanes] * (
                masks[tap_count - 1 - tap] * moved
            )
        out[:, lanes] = total.astype(BF16)


def spread(conv_grad, kernel, masks):
    vmem = pl.BlockSpec(memory_space=pltpu.VMEM)
    return pl.pallas_call(
        spread_kernel,
        out_shape=jax.ShapeDtypeStruct((conv_grad.shape[0] - 2 * EDGE, kernel.shape[1]), BF16),
        in_specs=[vmem] * 3,
        out_specs=vmem,
        compiler_params=pltpu.CompilerParams(vmem_limit_bytes=12 << 20),
        cost_estimate=pl.CostEstimate(flops=6_000_000_000, bytes_accessed=3_000_000, transcendentals=0),
        name="spread",
    )(conv_grad, kernel, masks)


def local(
    glu_frames,
    residual_frames,
    send_rows,
    recv_slot,
    segment_ids,
    code_targets,
    conv_kernel,
    norm_gain,
    point_weight,
    code_head,
):
    n_dp, n_fsdp = lax.axis_size("dp"), lax.axis_size("fsdp")
    d, f = lax.axis_index("dp"), lax.axis_index("fsdp")
    feature_width = glu_frames.shape[1]
    tap_count = conv_kernel.shape[0]
    half_taps = tap_count // 2
    slot_list = recv_slot[0, 0]
    row_count = slot_list.shape[0]
    picked_rows = send_rows[0, 0]

    capacity = picked_rows.shape[1]
    sent = jnp.concatenate([glu_frames[picked_rows], residual_frames[picked_rows]], axis=1)
    received = lax.all_to_all(sent, "dp", split_axis=0, concat_axis=0, tiled=True)
    segments = segment_ids[0, 0]
    seg_pad = jnp.pad(segments, (half_taps, half_taps), constant_values=-1)
    masks = jnp.stack(
        [seg_pad[offset : offset + row_count] == segments for offset in range(tap_count)]
    )
    masks = jnp.broadcast_to(masks.astype(F32)[:, :, None], (*masks.shape, 128))
    glu_owned, residual_owned, standard, inv_std, activation = forward(
        received, slot_list, masks, conv_kernel, norm_gain
    )

    pieces = gather_point(point_weight, d, activation)
    full_panel, residual_new = branch(
        point_weight, activation, residual_owned, pieces, d, f
    )

    code_local = code_head.shape[1]
    targets = code_targets[0].reshape(n_fsdp, row_count) - f * code_local
    columns = lax.broadcasted_iota(jnp.int32, (1, code_local), 1)
    gathered = gather_rows(residual_new, f)
    logits, hits, stats = {}, {}, {}
    act_own = after(activation, residual_new)
    acts = {mask: flip_dp(act_own, mask) if mask else act_own for mask in range(0, n_dp, 2)}
    acts.update({mask + 1: flip_dp(act, 1) for mask, act in list(acts.items())})
    gathered[-1] = (gathered[-1][0], after(gathered[-1][1], *acts.values()))
    for distance, block in gathered:
        logits[distance] = jnp.dot(block, code_head, preferred_element_type=F32)
        hits[distance] = pick(targets, (f + distance) % n_fsdp)[:, None] == columns
        top = jnp.max(logits[distance], axis=1)
        total = jnp.sum(jnp.exp(logits[distance] - top[:, None]), axis=1)
        chosen = jnp.sum(jnp.where(hits[distance], logits[distance], 0.0), axis=1)
        stats[distance] = jnp.stack([top, total, chosen])
    places = jnp.arange(n_fsdp)[:, None, None]
    table = tree_sum(
        [
            jnp.where(places == (f + distance) % n_fsdp, stats[distance], 0.0)
            for distance, _ in gathered
        ]
    )
    tables = [table] + [flip_fsdp(table, mask) for mask in range(1, n_fsdp)]
    tops = tables[0][:, 0]
    for other in tables[1:]:
        tops = jnp.maximum(tops, other[:, 0])
    sums = tree_sum([t[:, 1] * jnp.exp(t[:, 0] - tops) for t in tables])
    log_norm = tops + jnp.log(sums)
    loss_part = jnp.sum(log_norm - tree_sum([t[:, 2] for t in tables]))

    def code_part(distances, dtype):
        index = jnp.stack([(f + distance) % n_fsdp for distance in distances])
        return code_grad(
            [logits[distance] for distance in distances],
            index,
            log_norm,
            targets,
            code_head,
            dtype,
        )

    grad_residual, sides = scatter_rows(code_part, gathered, d, f)
    grad_residual, turned = lax.optimization_barrier(
        (grad_residual.astype(BF16), grad_residual.astype(BF16).T)
    )

    part_width = feature_width // n_dp
    cols = lax.all_to_all(
        turned.reshape(n_dp, part_width, row_count),
        "dp",
        split_axis=0,
        concat_axis=0,
        tiled=True,
    )
    core = d & 1
    packet, packet_sent, conv_grad = taps(
        grad_residual,
        full_panel,
        standard,
        inv_std,
        norm_gain,
        glu_owned,
        masks,
        loss_part.reshape(1, 1),
        core,
    )

    packet = packet + flip_dp(after(packet_sent, cols), 1).astype(F32)
    packet = packet.astype(BF16)
    cols = after(cols, packet)
    point_own, *point_sent = point_part(cols, [acts[mask] for mask in range(n_dp)], d, f)
    sides = [(keep, after(other, *point_sent), left) for keep, other, left in sides]
    sides = middle_folds(sides, d)
    ready = [keep for keep, _, _ in sides]
    others = [after(flip_dp(packet, mask), *ready) for mask in range(2, n_dp, 2)]
    packet = tree_sum([packet.astype(F32)] + [other.astype(F32) for other in others])
    packet = packet.astype(BF16)
    grad_point = tree_sum(
        [point_own]
        + [
            flip_fsdp(after(sent, packet), mask + 1).astype(F32)
            for mask, sent in enumerate(point_sent)
        ]
    ).T
    grad_glu = spread(after(conv_grad, packet), conv_kernel, masks)
    grad_head = last_fold([after(part, packet, grad_point) for keep, other, _ in sides for part in (keep, other)])
    others = [
        after(flip_fsdp(packet, mask), grad_glu, grad_head) for mask in range(1, n_fsdp)
    ]
    packet = tree_sum([packet.astype(F32)] + [other.astype(F32) for other in others])
    packet = ordered(core, packet, flip_dp(packet, 1), 1).reshape(-1, feature_width)
    loss = packet[tap_count + 1, 0] / (row_count * n_dp * n_fsdp * n_fsdp)
    return (
        loss,
        grad_head,
        grad_point,
        packet[:tap_count],
        packet[tap_count],
        grad_residual,
        grad_glu,
    )


def solution(mesh):
    placed = (
        P(("dp", "fsdp"), None),
        P(("dp", "fsdp"), None),
        P("dp", "fsdp", None, None),
        P("dp", "fsdp", None),
        P("dp", "fsdp", None),
        P("dp", None),
        P(),
        P(),
        P("fsdp", None),
        P(None, "fsdp"),
    )
    return jax.shard_map(
        local,
        mesh=mesh,
        in_specs=placed,
        out_specs=(
            P(),
            P("dp", "fsdp"),
            P("fsdp", "dp"),
            P(),
            P(),
            P(("dp", "fsdp"), None),
            P(("dp", "fsdp"), None),
        ),
        check_vma=False,
    )
```

```python
import functools

import jax
import jax.numpy as jnp
from jax import lax
from jax.experimental import pallas as pl
from jax.experimental.pallas import tpu as pltpu
from jax.sharding import PartitionSpec as P

F32 = jnp.float32
BF16 = jnp.bfloat16


def flip_dp(value, mask):
    count = lax.axis_size("dp")
    return lax.ppermute(value, "dp", [(i, i ^ mask) for i in range(count)])


def flip_fsdp(value, mask):
    count = lax.axis_size("fsdp")
    return lax.ppermute(value, "fsdp", [(i, i ^ mask) for i in range(count)])


def shift_fsdp(value, step):
    count = lax.axis_size("fsdp")
    return lax.ppermute(value, "fsdp", [(i, (i + step) % count) for i in range(count)])


def pick(array, index, axis=0):
    return lax.dynamic_index_in_dim(array, index, axis, keepdims=False)


def ordered(bit, own, other, axis):
    return jnp.where(
        bit == 0, jnp.stack([own, other], axis), jnp.stack([other, own], axis)
    )


def tree_sum(values):
    while len(values) > 1:
        values = [values[i] + values[i + 1] for i in range(0, len(values), 2)]
    return values[0]


def after(value, *others):
    return lax.optimization_barrier((value, *others))[0]


def gather_point(point_weight, d, activation):
    count = lax.axis_size("fsdp")
    rows, width = point_weight.shape
    core, bit1, bit2 = d & 1, (d >> 1) & 1, (d >> 2) & 1
    parts = point_weight.reshape(2, 2, 2, rows // 8, width)
    piece1 = pick(pick(parts[0], bit1), core)
    piece2 = pick(pick(parts[1], bit2), core)
    piece = jnp.stack([piece1, piece2])
    got = jnp.stack([shift_fsdp(piece, step) for step in range(1, count)], 1)
    across = [flip_dp(got[0], 2), flip_dp(got[1], 4)]
    far = [flip_dp(got, 1)] + [flip_dp(after(piece, activation), 1) for piece in across]
    return [got] + across + far


def branch_kernel(
    place, weight, act, residual, got, got1, got2, far, far1, far2, kept, out, panel, sems, keep
):
    count = panel.shape[0]
    d, f = place[0], place[1]
    core, bits = d & 1, ((d >> 1) & 1, (d >> 2) & 1)
    copies = [(weight, panel.at[f])]
    for step in range(1, count):
        shard = panel.at[lax.rem(f + count - step, count)]
        for mine, others, side in (
            (got, (got1, got2), core),
            (far, (far1, far2), 1 - core),
        ):
            for half in range(2):
                copies.append((mine.at[half, step - 1], shard.at[half, bits[half], side]))
                copies.append((others[half].at[step - 1], shard.at[half, 1 - bits[half], side]))
    copies = [
        pltpu.make_async_copy(source, target, sems.at[i])
        for i, (source, target) in enumerate(copies)
    ]
    for copy in copies:
        copy.start()
    for copy in copies:
        copy.wait()
    keeping = pltpu.make_async_copy(panel, kept, keep)
    keeping.start()
    rows, width = act.shape
    tile = 512
    whole = panel.reshape(act.shape[1], width)

    @pl.loop(0, width // tile)
    def _(step):
        lanes = pl.ds(pl.multiple_of(step * tile, tile), tile)
        total = jnp.dot(act[...], whole[:, lanes], preferred_element_type=F32)
        out[:, lanes] = (residual[:, lanes].astype(F32) + total).astype(BF16)

    keeping.wait()


def branch(point_weight, activation, residual_owned, pieces, d, f):
    count = lax.axis_size("fsdp")
    rows, width = point_weight.shape
    vmem = pl.BlockSpec(memory_space=pltpu.VMEM)
    panel, out = pl.pallas_call(
        branch_kernel,
        out_shape=(
            jax.ShapeDtypeStruct((count, 2, 2, 2, rows // 8, width), BF16),
            jax.ShapeDtypeStruct(activation.shape, BF16),
        ),
        in_specs=[pl.BlockSpec(memory_space=pltpu.SMEM), pl.BlockSpec(memory_space=pltpu.HBM)]
        + [vmem] * 2
        + [pl.BlockSpec(memory_space=pl.ANY)] * 6,
        out_specs=(pl.BlockSpec(memory_space=pltpu.HBM), vmem),
        scratch_shapes=[
            pltpu.VMEM((count, 2, 2, 2, rows // 8, width), BF16),
            pltpu.SemaphoreType.DMA((1 + 8 * (count - 1),)),
            pltpu.SemaphoreType.DMA,
        ],
        compiler_params=pltpu.CompilerParams(vmem_limit_bytes=60 << 20),
        name="branch",
    )(
        jnp.stack([d, f]),
        point_weight.reshape(2, 2, 2, rows // 8, width),
        activation,
        residual_owned,
        *pieces,
    )
    return panel.reshape(count * rows, width), out


EDGE = 16


def forward_kernel(
    sent, slots, masks, kernel, gain, glu, residual, standard, inv_std, act, padded, received, sem
):
    copy = pltpu.make_async_copy(sent, received, sem)
    copy.start()
    rows, width = standard.shape
    tap_count = masks.shape[0]
    half_taps = tap_count // 2
    loaders, both, _ = received.shape
    capacity = both // 2
    places = lax.broadcasted_iota(jnp.int32, (rows, loaders * capacity), 1)
    chosen = (slots[...] == places).astype(BF16)
    tile = 512
    tiles = [slice(i, i + tile) for i in range(0, width, tile)]
    for edge in (0, EDGE + rows):
        padded[pl.ds(edge, EDGE), :] = jnp.zeros((EDGE, width), F32)
    copy.wait()
    for lanes in tiles:
        for start, target in ((0, glu), (capacity, residual)):
            frames = received[:, start : start + capacity, lanes]
            frames = frames.reshape(loaders * capacity, tile)
            owned = jnp.dot(chosen, frames, preferred_element_type=F32)
            target[:, lanes] = owned.astype(BF16)
            if start == 0:
                padded[pl.ds(EDGE, rows), lanes] = owned

    @pl.loop(0, width // 128)
    def _(step):
        lanes = pl.ds(pl.multiple_of(step * 128, 128), 128)
        total = jnp.zeros((rows, 128), F32)
        for tap in range(tap_count):
            moved = padded[pl.ds(EDGE + tap - half_taps, rows), lanes]
            total = total + kernel[pl.ds(tap, 1), lanes] * (masks[tap] * moved)
        standard[:, lanes] = total

    mean = sum(jnp.sum(standard[:, lanes], axis=1, keepdims=True) for lanes in tiles) / width
    square = jnp.zeros((rows, 1), F32)
    for lanes in tiles:
        centred = standard[:, lanes] - mean
        square = square + jnp.sum(centred * centred, axis=1, keepdims=True)
    scale = lax.rsqrt(square / width + 1e-05)
    inv_std[...] = scale
    for lanes in tiles:
        unit = (standard[:, lanes] - mean) * scale
        standard[:, lanes] = unit
        normed = unit * gain[:, lanes]
        act[:, lanes] = (normed * jax.nn.sigmoid(normed)).astype(BF16)


def forward(received, slot_list, masks, kernel, gain):
    rows, width = slot_list.shape[0], received.shape[2]
    vmem = pl.BlockSpec(memory_space=pltpu.VMEM)
    half = jax.ShapeDtypeStruct((rows, width), BF16)
    return pl.pallas_call(
        forward_kernel,
        out_shape=(
            half,
            half,
            jax.ShapeDtypeStruct((rows, width), F32),
            jax.ShapeDtypeStruct((rows, 1), F32),
            half,
        ),
        in_specs=[pl.BlockSpec(memory_space=pltpu.HBM)] + [vmem] * 4,
        out_specs=(vmem,) * 5,
        scratch_shapes=[
            pltpu.VMEM((rows + 2 * EDGE, width), F32),
            pltpu.VMEM(received.shape, BF16),
            pltpu.SemaphoreType.DMA,
        ],
        compiler_params=pltpu.CompilerParams(vmem_limit_bytes=60 << 20),
        cost_estimate=pl.CostEstimate(
            flops=1_000_000_000, bytes_accessed=6_000_000, transcendentals=200_000
        ),
        name="forward",
    )(received, slot_list[:, None], masks, kernel, gain[None, :])


def code_kernel(count, index, norms, targets, *refs):
    logits, head = refs[:count], refs[count]
    grads, outs = refs[count + 1 : 2 * count + 1], refs[2 * count + 1 : 3 * count + 1]
    norm, target, total, held, sems = refs[3 * count + 1 :]
    rows, codes = logits[0].shape
    parts, _, tile = held.shape
    copies = [
        pltpu.make_async_copy(head.at[:, pl.ds(i * tile, tile)], held.at[i], sems.at[i])
        for i in range(parts)
    ]
    for copy in copies:
        copy.start()
    for i in range(count):
        for table, column in ((norms, norm), (targets, target)):
            line = table[pl.ds(index[i], 1), :]
            column[i] = jnp.broadcast_to(line, (rows, rows)).T
    for part in range(parts):
        lanes = slice(part * tile, (part + 1) * tile)
        columns = lax.broadcasted_iota(jnp.int32, (rows, tile), 1) + part * tile
        values = []
        for i in range(count):
            hits = (columns == target[i][:, :1].astype(jnp.int32)).astype(F32)
            value = (jnp.exp(logits[i][:, lanes] - norm[i][:, :1]) - hits).astype(BF16)
            grads[i][:, lanes] = value
            values.append(value)
        value = jnp.concatenate(values) if count > 1 else values[0]
        copies[part].wait()
        product = lax.dot_general(
            value, held[part], (((1,), (1,)), ((), ())), preferred_element_type=F32
        )
        if part:
            product = total[...] + product
        if part < parts - 1:
            total[...] = product
        else:
            for i in range(count):
                outs[i][...] = product[i * rows : (i + 1) * rows].astype(outs[i].dtype)


def code_grad(logits, index, norms, targets, head, dtype):
    count = len(logits)
    rows, codes = logits[0].shape
    width, tile = head.shape[0], 512
    vmem = pl.BlockSpec(memory_space=pltpu.VMEM)
    made = pl.pallas_call(
        functools.partial(code_kernel, count),
        out_shape=[jax.ShapeDtypeStruct((rows, codes), BF16)] * count
        + [jax.ShapeDtypeStruct((rows, width), dtype)] * count,
        in_specs=[pl.BlockSpec(memory_space=pltpu.SMEM)]
        + [vmem] * (count + 2)
        + [pl.BlockSpec(memory_space=pltpu.HBM)],
        out_specs=[vmem] * (2 * count),
        scratch_shapes=[
            pltpu.VMEM((count, rows, rows), F32),
            pltpu.VMEM((count, rows, rows), F32),
            pltpu.VMEM((count * rows, width), F32),
            pltpu.VMEM((codes // tile, width, tile), BF16),
            pltpu.SemaphoreType.DMA((codes // tile,)),
        ],
        compiler_params=pltpu.CompilerParams(vmem_limit_bytes=(10 + 4 * count) << 20),
        cost_estimate=pl.CostEstimate(
            flops=800_000_000 * count, bytes_accessed=8_000_000, transcendentals=200_000 * count
        ),
        name="code",
    )(index, norms, targets.astype(F32), *logits, head)
    return made[:count], made[count:]


def point_kernel(count, place, cols, *refs):
    given = refs[:count]
    own, outs = refs[count], refs[count + 1 : -3]
    acts, parts, sems = refs[-3:]
    d, f = place[0], place[1]
    copies = [pltpu.make_async_copy(given[i], acts.at[i], sems.at[i]) for i in range(count)]
    for copy in copies:
        copy.start()
    for copy in copies:
        copy.wait()
    blocks, _, width = parts.shape
    for block in range(blocks):
        lanes = slice(block * width, (block + 1) * width)
        total = jnp.zeros(own.shape, F32)
        for mask in range(count):
            total = total + jnp.dot(
                cols[d ^ mask], acts[mask, :, lanes], preferred_element_type=F32
            )
        parts[block] = total
    own[...] = parts[f]
    for i, out in enumerate(outs):
        out[...] = parts[f ^ (i + 1)].astype(BF16)


def point_part(cols, acts, d, f):
    n_fsdp = lax.axis_size("fsdp")
    width = acts[0].shape[1] // n_fsdp
    vmem = pl.BlockSpec(memory_space=pltpu.VMEM)
    return pl.pallas_call(
        functools.partial(point_kernel, len(acts)),
        out_shape=[jax.ShapeDtypeStruct((cols.shape[1], width), F32)]
        + [jax.ShapeDtypeStruct((cols.shape[1], width), BF16)] * (n_fsdp - 1),
        in_specs=[pl.BlockSpec(memory_space=pltpu.SMEM), vmem]
        + [pl.BlockSpec(memory_space=pltpu.HBM)] * len(acts),
        out_specs=[vmem] * n_fsdp,
        scratch_shapes=[
            pltpu.VMEM((len(acts), *acts[0].shape), BF16),
            pltpu.VMEM((n_fsdp, cols.shape[1], width), F32),
            pltpu.SemaphoreType.DMA((len(acts),)),
        ],
        compiler_params=pltpu.CompilerParams(vmem_limit_bytes=60 << 20),
        cost_estimate=pl.CostEstimate(flops=1000, bytes_accessed=1000, transcendentals=0),
        name="point",
    )(jnp.stack([d, f]), cols, *acts)


def gather_rows(own, f):
    count = lax.axis_size("fsdp")
    if count != 4:
        return [(0, own)] + [(count - step, shift_fsdp(own, step)) for step in range(1, count)]
    before = shift_fsdp(own, 1)
    after = shift_fsdp(own, -1)
    source = jnp.where(f == 2, before, jnp.where(f == 1, after, own))
    across = lax.ppermute(source, "fsdp", [(0, 2), (3, 1), (2, 3), (1, 0)])
    return [(0, own), (3, before), (1, after), (2, across)]


def scatter_rows(code_part, gathered, d, f):
    count = lax.axis_size("fsdp")

    places = [distance for distance, _ in gathered]

    def head_grad(grads):
        return lax.dot_general(
            jnp.concatenate([block for _, block in gathered]),
            jnp.concatenate([grads[place] for place in places]),
            (((0,), (0,)), ((), ())),
            preferred_element_type=F32,
        ).astype(BF16)

    if count != 4:
        grads, outs = code_part(places, F32)
        grads, outs = dict(zip(places, grads)), dict(zip(places, outs))
        got = [shift_fsdp(outs[step].astype(BF16), step).astype(F32) for step in range(1, count)]
        return sum(got, outs[0]), join_cores(head_grad(grads), None, d)
    grads = {}
    (grads[2],), (block,) = code_part([2], BF16)
    across = lax.ppermute(block, "fsdp", [(2, 0), (1, 3), (3, 2), (0, 1)])
    (grads[1], grads[3], grads[0]), (ahead, behind, own) = code_part([1, 3, 0], F32)
    head = head_grad(grads)
    sent = other_core(head, d)
    across = after(across, own, sent).astype(F32)
    ahead = (ahead + jnp.where(f == 1, across, 0.0)).astype(BF16)
    behind = (behind + jnp.where(f == 2, across, 0.0)).astype(BF16)
    got1 = shift_fsdp(ahead, 1)
    got2 = shift_fsdp(behind, -1)
    direct = jnp.where((f == 0) | (f == 3), across, 0.0)
    sides = join_cores(head, after(sent, ahead, behind), d)
    got1 = after(got1, *[keep for keep, _, _ in sides])
    return own + direct + got1.astype(F32) + got2.astype(F32), sides


def fold_kernel(cut, place, *refs):
    ins, outs, held, sems = refs[:4], refs[4:8], refs[8:12], refs[12]
    copies = []
    for i, (source, target) in enumerate(zip(ins, held)):
        if cut:
            width = target.shape[-1]
            lanes = pl.ds(i // 2 * width, width)
            if i % 2:
                source = source.at[:, :, :, :, lanes]
            else:
                source = source.at[:, :, :, place[2], :, lanes]
        copies.append(pltpu.make_async_copy(source, target, sems.at[i]))
        copies[-1].start()
    for side in range(2):
        own, other = held[2 * side], held[2 * side + 1]
        copies[2 * side].wait()
        copies[2 * side + 1].wait()
        keep, send = outs[2 * side], outs[2 * side + 1]
        before, _, behind = own.shape[:3]
        for first in range(before):
            for last in range(behind):
                for target, half in ((keep, place[side]), (send, 1 - place[side])):
                    total = own[first, half, last].astype(F32) + other[first, half, last].astype(F32)
                    target[first, last] = total.astype(target.dtype)


def fold(sides, d, cut=False):
    ins, outs, held, left_over = [], [], [], []
    for own, other, left, bit in sides:
        place = left.index(bit)
        rows, width = other.shape[-2:]
        part = width // 2 if cut else width
        before, behind = 2**place, 2 ** (len(left) - 1 - place)
        cores = (2,) if cut else ()
        ins.append(own.reshape(before, 2, behind, *cores, rows, width))
        ins.append(other.reshape(before, 2, behind, rows, width))
        held += [pltpu.VMEM((before, 2, behind, rows, part), BF16)] * 2
        outs += [jax.ShapeDtypeStruct((before, behind, rows, part), BF16)] * 2
        left_over.append([b for b in left if b != bit])
    vmem = pl.BlockSpec(memory_space=pltpu.VMEM)
    made = pl.pallas_call(
        functools.partial(fold_kernel, cut),
        out_shape=outs,
        in_specs=[pl.BlockSpec(memory_space=pltpu.SMEM)] + [pl.BlockSpec(memory_space=pl.ANY)] * 4,
        out_specs=[vmem] * 4,
        scratch_shapes=held + [pltpu.SemaphoreType.DMA((4,))],
        compiler_params=pltpu.CompilerParams(vmem_limit_bytes=16 << 20),
        cost_estimate=pl.CostEstimate(flops=1000, bytes_accessed=1000, transcendentals=0),
        name="fold",
    )(jnp.stack([(d >> side[3]) & 1 for side in sides] + [d & 1]), *ins)
    return [(made[2 * i], made[2 * i + 1], left_over[i]) for i in range(2)]


def last_kernel(*refs):
    out = refs[4]
    width = refs[0].shape[-1]
    for side in range(2):
        total = refs[2 * side][...].astype(F32) + refs[2 * side + 1][...].astype(F32)
        out[:, side * width : (side + 1) * width] = total


def last_fold(parts):
    rows, width = parts[0].shape[-2:]
    vmem = pl.BlockSpec(memory_space=pltpu.VMEM)
    return pl.pallas_call(
        last_kernel,
        out_shape=jax.ShapeDtypeStruct((rows, 2 * width), F32),
        in_specs=[vmem] * 4,
        out_specs=vmem,
        compiler_params=pltpu.CompilerParams(vmem_limit_bytes=12 << 20),
        cost_estimate=pl.CostEstimate(flops=1000, bytes_accessed=1000, transcendentals=0),
        name="last",
    )(*[part.reshape(rows, width) for part in parts])


def halve_bits(step):
    bits = lax.axis_size("dp").bit_length() - 1
    return [list(range(1, bits))[step], list(range(bits - 1, 0, -1))[step]]


def by_core(head):
    count = lax.axis_size("dp")
    return head.reshape(count // 2, 2, head.shape[0] // count, head.shape[1])


def other_core(head, d):
    return pick(by_core(head), 1 - (d & 1), 1)


def join_cores(head, sent, d):
    count = lax.axis_size("dp")
    left = list(range(count.bit_length() - 2, 0, -1))
    cut = by_core(head)
    got = flip_dp(other_core(head, d) if sent is None else sent, 1)
    sides = [(cut, got, left, bit) for bit in halve_bits(0)]
    return send_on(fold(sides, d, True), 0)


def send_on(folded, step):
    return [
        (keep, flip_dp(send, 1 << bit), left)
        for (keep, send, left), bit in zip(folded, halve_bits(step))
    ]


def middle_folds(sides, d):
    bits = lax.axis_size("dp").bit_length() - 1
    for step in range(1, bits - 1):
        ready = [(*side, bit) for side, bit in zip(sides, halve_bits(step))]
        sides = send_on(fold(ready, d), step)
    return sides


def taps_kernel(
    grad, panel, standard, inv_std, gain, glu, masks, loss, place, mine, sent, conv_grad, scaled, padded, packet, *held
):
    rows, width = standard.shape
    tap_count = masks.shape[0]
    half_taps = tap_count // 2
    tile = 512
    panel_held, standard_held, glu_held, masks_held, sems = held
    copies = [
        pltpu.make_async_copy(source, target, sems.at[i])
        for i, (source, target) in enumerate(
            [(standard, standard_held)]
            + [
                (panel.at[pl.ds(i * tile, tile)], panel_held.at[pl.ds(i * tile, tile)])
                for i in range(width // tile)
            ]
            + [(glu, glu_held), (masks, masks_held)]
        )
    ]
    for copy in copies:
        copy.start()
    panel, standard, glu, masks = panel_held, standard_held, glu_held, masks_held
    copies[0].wait()
    parts = packet.shape[2] // 128
    rest = packet.shape[1] - tap_count - 1
    packet[:, pl.ds(tap_count + 1, rest), :] = jnp.full((2, rest, packet.shape[2]), loss[0, 0])
    sums = jnp.zeros((rows, 1), F32)
    dots = jnp.zeros((rows, 1), F32)
    for lanes in [slice(i, i + tile) for i in range(0, width, tile)]:
        copies[1 + lanes.start // tile].wait()
        act_grad = lax.dot_general(
            grad[...], panel[lanes, :], (((1,), (1,)), ((), ())), preferred_element_type=F32
        )
        scale = gain[:, lanes]
        unit = standard[:, lanes]
        normed = unit * scale
        sig = jax.nn.sigmoid(normed)
        normed_grad = act_grad * sig * (1.0 + normed * (1.0 - sig))
        gain_grad = jnp.sum(normed_grad * unit, axis=0, keepdims=True)
        for first in range(0, tile, 128):
            half, first_lane = divmod(lanes.start + first, packet.shape[2])
            packet[half, pl.ds(tap_count, 1), first_lane : first_lane + 128] = gain_grad[
                :, first : first + 128
            ]
        part = normed_grad * scale
        scaled[:, lanes] = part
        sums = sums + jnp.sum(part, axis=1, keepdims=True)
        dots = dots + jnp.sum(part * unit, axis=1, keepdims=True)
    for copy in copies[-2:]:
        copy.wait()
    sums, dots, scale = sums / width, dots / width, inv_std[...]
    for edge in (0, EDGE + rows):
        conv_grad[pl.ds(edge, EDGE), :] = jnp.zeros((EDGE, width), F32)
        padded[pl.ds(edge, EDGE), :] = jnp.zeros((EDGE, width), F32)
    for lanes in [slice(i, i + tile) for i in range(0, width, tile)]:
        conv_grad[pl.ds(EDGE, rows), lanes] = scale * (
            scaled[:, lanes] - sums - standard[:, lanes] * dots
        )
        padded[pl.ds(EDGE, rows), lanes] = glu[:, lanes].astype(F32)

    @pl.loop(0, width // 128)
    def _(step):
        lanes = pl.ds(pl.multiple_of(step * 128, 128), 128)
        there = pl.ds(pl.multiple_of(lax.rem(step, parts) * 128, 128), 128)
        value = conv_grad[pl.ds(EDGE, rows), lanes]
        for tap in range(tap_count):
            moved = padded[pl.ds(EDGE + tap - half_taps, rows), lanes]
            packet[step // parts, pl.ds(tap, 1), there] = jnp.sum(
                value * (masks[tap] * moved), axis=0, keepdims=True
            )

    mine[...] = packet[place[0]]
    sent[...] = packet[1 - place[0]].astype(BF16)


def taps(grad, panel, standard, inv_std, gain, glu, masks, loss, core):
    rows, width = standard.shape
    whole = pl.BlockSpec(memory_space=pltpu.HBM)
    half = ((masks.shape[0] + 9) // 8 * 8, width // 2)
    vmem = pl.BlockSpec(memory_space=pltpu.VMEM)
    return pl.pallas_call(
        taps_kernel,
        out_shape=(
            jax.ShapeDtypeStruct(half, F32),
            jax.ShapeDtypeStruct(half, BF16),
            jax.ShapeDtypeStruct((rows + 2 * EDGE, width), F32),
        ),
        in_specs=[vmem, whole, whole, vmem, vmem, whole, whole]
        + [pl.BlockSpec(memory_space=pltpu.SMEM)] * 2,
        out_specs=(vmem,) * 3,
        scratch_shapes=[
            pltpu.VMEM((rows, width), F32),
            pltpu.VMEM((rows + 2 * EDGE, width), F32),
            pltpu.VMEM((2, *half), F32),
            pltpu.VMEM(panel.shape, BF16),
            pltpu.VMEM(standard.shape, F32),
            pltpu.VMEM(glu.shape, BF16),
            pltpu.VMEM(masks.shape, F32),
            pltpu.SemaphoreType.DMA((3 + width // 512,)),
        ],
        compiler_params=pltpu.CompilerParams(vmem_limit_bytes=60 << 20),
        cost_estimate=pl.CostEstimate(flops=1000, bytes_accessed=1000, transcendentals=0),
        name="taps",
    )(grad, panel, standard, inv_std, gain[None, :], glu, masks, loss, core[None])


def spread_kernel(conv_grad, kernel, masks, out):
    rows, width = out.shape
    tap_count = masks.shape[0]
    half_taps = tap_count // 2

    @pl.loop(0, width // 128)
    def _(step):
        lanes = pl.ds(pl.multiple_of(step * 128, 128), 128)
        total = jnp.zeros((rows, 128), F32)
        for tap in range(tap_count):
            moved = conv_grad[pl.ds(EDGE + half_taps - tap, rows), lanes]
            total = total + kernel[pl.ds(tap, 1), lanes] * (
                masks[tap_count - 1 - tap] * moved
            )
        out[:, lanes] = total.astype(BF16)


def spread(conv_grad, kernel, masks):
    vmem = pl.BlockSpec(memory_space=pltpu.VMEM)
    return pl.pallas_call(
        spread_kernel,
        out_shape=jax.ShapeDtypeStruct((conv_grad.shape[0] - 2 * EDGE, kernel.shape[1]), BF16),
        in_specs=[vmem] * 3,
        out_specs=vmem,
        compiler_params=pltpu.CompilerParams(vmem_limit_bytes=12 << 20),
        cost_estimate=pl.CostEstimate(flops=6_000_000_000, bytes_accessed=3_000_000, transcendentals=0),
        name="spread",
    )(conv_grad, kernel, masks)


def local(
    glu_frames,
    residual_frames,
    send_rows,
    recv_slot,
    segment_ids,
    code_targets,
    conv_kernel,
    norm_gain,
    point_weight,
    code_head,
):
    n_dp, n_fsdp = lax.axis_size("dp"), lax.axis_size("fsdp")
    d, f = lax.axis_index("dp"), lax.axis_index("fsdp")
    feature_width = glu_frames.shape[1]
    tap_count = conv_kernel.shape[0]
    half_taps = tap_count // 2
    slot_list = recv_slot[0, 0]
    row_count = slot_list.shape[0]
    picked_rows = send_rows[0, 0]

    capacity = picked_rows.shape[1]
    sent = jnp.concatenate([glu_frames[picked_rows], residual_frames[picked_rows]], axis=1)
    received = lax.all_to_all(sent, "dp", split_axis=0, concat_axis=0, tiled=True)
    segments = segment_ids[0, 0]
    seg_pad = jnp.pad(segments, (half_taps, half_taps), constant_values=-1)
    masks = jnp.stack(
        [seg_pad[offset : offset + row_count] == segments for offset in range(tap_count)]
    )
    masks = jnp.broadcast_to(masks.astype(F32)[:, :, None], (*masks.shape, 128))
    glu_owned, residual_owned, standard, inv_std, activation = forward(
        received, slot_list, masks, conv_kernel, norm_gain
    )

    pieces = gather_point(point_weight, d, activation)
    full_panel, residual_new = branch(
        point_weight, activation, residual_owned, pieces, d, f
    )

    code_local = code_head.shape[1]
    targets = code_targets[0].reshape(n_fsdp, row_count) - f * code_local
    columns = lax.broadcasted_iota(jnp.int32, (1, code_local), 1)
    gathered = gather_rows(residual_new, f)
    logits, hits, stats = {}, {}, {}
    act_own = after(activation, residual_new)
    acts = {mask: flip_dp(act_own, mask) if mask else act_own for mask in range(0, n_dp, 2)}
    acts.update({mask + 1: flip_dp(act, 1) for mask, act in list(acts.items())})
    gathered[-1] = (gathered[-1][0], after(gathered[-1][1], *acts.values()))
    for distance, block in gathered:
        logits[distance] = jnp.dot(block, code_head, preferred_element_type=F32)
        hits[distance] = pick(targets, (f + distance) % n_fsdp)[:, None] == columns
        top = jnp.max(logits[distance], axis=1)
        total = jnp.sum(jnp.exp(logits[distance] - top[:, None]), axis=1)
        chosen = jnp.sum(jnp.where(hits[distance], logits[distance], 0.0), axis=1)
        stats[distance] = jnp.stack([top, total, chosen])
    places = jnp.arange(n_fsdp)[:, None, None]
    table = tree_sum(
        [
            jnp.where(places == (f + distance) % n_fsdp, stats[distance], 0.0)
            for distance, _ in gathered
        ]
    )
    tables = [table] + [flip_fsdp(table, mask) for mask in range(1, n_fsdp)]
    tops = tables[0][:, 0]
    for other in tables[1:]:
        tops = jnp.maximum(tops, other[:, 0])
    sums = tree_sum([t[:, 1] * jnp.exp(t[:, 0] - tops) for t in tables])
    log_norm = tops + jnp.log(sums)
    loss_part = jnp.sum(log_norm - tree_sum([t[:, 2] for t in tables]))

    def code_part(distances, dtype):
        index = jnp.stack([(f + distance) % n_fsdp for distance in distances])
        return code_grad(
            [logits[distance] for distance in distances],
            index,
            log_norm,
            targets,
            code_head,
            dtype,
        )

    grad_residual, sides = scatter_rows(code_part, gathered, d, f)
    grad_residual, turned = lax.optimization_barrier(
        (grad_residual.astype(BF16), grad_residual.astype(BF16).T)
    )

    part_width = feature_width // n_dp
    cols = lax.all_to_all(
        turned.reshape(n_dp, part_width, row_count),
        "dp",
        split_axis=0,
        concat_axis=0,
        tiled=True,
    )
    core = d & 1
    packet, packet_sent, conv_grad = taps(
        grad_residual,
        full_panel,
        standard,
        inv_std,
        norm_gain,
        glu_owned,
        masks,
        loss_part.reshape(1, 1),
        core,
    )

    packet = packet + flip_dp(after(packet_sent, cols), 1).astype(F32)
    packet = packet.astype(BF16)
    cols = after(cols, packet)
    point_own, *point_sent = point_part(cols, [acts[mask] for mask in range(n_dp)], d, f)
    sides = [(keep, after(other, *point_sent), left) for keep, other, left in sides]
    sides = middle_folds(sides, d)
    ready = [keep for keep, _, _ in sides]
    others = [after(flip_dp(packet, mask), *ready) for mask in range(2, n_dp, 2)]
    packet = tree_sum([packet.astype(F32)] + [other.astype(F32) for other in others])
    packet = packet.astype(BF16)
    grad_point = tree_sum(
        [point_own]
        + [
            flip_fsdp(after(sent, packet), mask + 1).astype(F32)
            for mask, sent in enumerate(point_sent)
        ]
    ).T
    grad_glu = spread(after(conv_grad, packet), conv_kernel, masks)
    grad_head = last_fold([after(part, packet, grad_point) for keep, other, _ in sides for part in (keep, other)])
    others = [
        after(flip_fsdp(packet, mask), grad_glu, grad_head) for mask in range(1, n_fsdp)
    ]
    packet = tree_sum([packet.astype(F32)] + [other.astype(F32) for other in others])
    packet = ordered(core, packet, flip_dp(packet, 1), 1).reshape(-1, feature_width)
    loss = packet[tap_count + 1, 0] / (row_count * n_dp * n_fsdp * n_fsdp)
    return (
        loss,
        grad_head,
        grad_point,
        packet[:tap_count],
        packet[tap_count],
        grad_residual,
        grad_glu,
    )


def solution(mesh):
    placed = (
        P(("dp", "fsdp"), None),
        P(("dp", "fsdp"), None),
        P("dp", "fsdp", None, None),
        P("dp", "fsdp", None),
        P("dp", "fsdp", None),
        P("dp", None),
        P(),
        P(),
        P("fsdp", None),
        P(None, "fsdp"),
    )
    return jax.shard_map(
        local,
        mesh=mesh,
        in_specs=placed,
        out_specs=(
            P(),
            P("dp", "fsdp"),
            P("fsdp", "dp"),
            P(),
            P(),
            P(("dp", "fsdp"), None),
            P(("dp", "fsdp"), None),
        ),
        check_vma=False,
    )
```
